32 devices in a mesh: groups: 2 (over x), tensor: 8 (over z, y), batch: 2 (over core).
Axes of the slice: x: 2, y: 2, z: 4, core: 2. Of those that a mesh axis runs over, the one named last changes fastest.
Arguments:
- hidden: bfloat16 [256, 2, 8192], P(('groups', 'tensor', 'batch')), parts along dimension 0, may hold values from -6 to 6
- wq: bfloat16 [8192, 8192], P(None, 'tensor'), may hold values from -0.0625 to 0.0625
- wkv: bfloat16 [8192, 2048], P(None, 'tensor'), may hold values from -0.0625 to 0.0625
- cache_pool: bfloat16 [512, 128, 2048], P(('groups', 'tensor', 'batch')), parts along dimension 0, may hold values from -240 to 240
- page_table: int32 [256, 2], P(('groups', 'tensor', 'batch')), parts along dimension 0, may hold values from 0 to 15, as said below
- ctx_len: int32 [256], P(('groups', 'tensor', 'batch')), parts along dimension 0, may hold values from 1 to 256
- prompt_slot: int32 [32], P(('groups', 'tensor', 'batch')), parts along dimension 0, may hold values from 0 to 7
- prompt_kv: bfloat16 [32, 128, 2048], P(('groups', 'batch'), None, 'tensor'), parts along dimension 0, may hold values from -6 to 6
Outputs:
- attended: bfloat16 [256, 2, 8192], P(('groups', 'tensor', 'batch')), parts along dimension 0
The draws below stay inside these ranges and needn't reach their ends.
There are 2 independent parts, one for each index of `groups`. The reference program is written for one: setup_inputs(seed, part) draws one part's arguments, and reference() takes and returns one part's arrays. A program takes and returns all parts, laid end to end along the dimension named above; an argument that names none is the same for every part. Nothing has to cross between parts.
Inputs may be any that keep to these rules, and one draw needn't show every extreme that they name: `page_table`: within each block of 8 sequences the entries name each of that block's 16 local pages exactly once; entry p holds the sequence's tokens p * 128 to (p + 1) * 128 - 1.
All inputs are finite; a program needn't handle non-finite values.
Results may differ from the reference program's by a relative error of at most 0.012.
Values may be sent and summed in bfloat16 or wider, within the bound.
No kernel may reach another device: no remote copies, remote signals or barrier semaphores. Data moves between devices by JAX's collectives and lax.ppermute only.
A program may use at most 128 MiB of HBM per device.

```python
import jax
import jax.numpy as jnp
from jax import lax

D = 8192
QUERY_HEADS = 64
KEY_VALUE_HEADS = 8
HEAD_SIZE = 128
PAGE = 128
SEQ_PAGES = 2
PLEN = 128
SEQ_DEV = 8
KEY_VALUE_WIDTH = 2048
POOL_DEV = 16
SEQS = 128
PROMPTS = 16
POOLS = 256
N_TENSOR = 8
N_BATCH = 2


def draw_cache_pool(key, part):
    base = jnp.clip(jax.random.normal(key, (POOLS, PAGE, KEY_VALUE_WIDTH), jnp.float32), -4.0, 4.0)
    return base.astype(jnp.bfloat16)


def draw_page_table(key, part):
    blocks = SEQS // SEQ_DEV
    subkeys = jax.random.split(jax.random.fold_in(key, 3), blocks)
    orders = jax.vmap(lambda single: jax.random.permutation(single, POOL_DEV))(subkeys)
    return orders.reshape(SEQS, SEQ_PAGES).astype(jnp.int32)


def touch_ends(values, key, low, high):
    longest = values.shape.index(max(values.shape))
    spots = []
    for shift in (0, 1):
        where = [jax.random.randint(jax.random.fold_in(key, axis), (), 0, length) for axis, length in enumerate(values.shape)]
        where[longest] = (where[longest] + shift) % values.shape[longest]
        spots.append(tuple(where))
    return values.at[spots[0]].set(low).at[spots[1]].set(high)


def block_scale(stream_key, shape, pieces, smallest, top_value):
    def one(dim, shards_of):
        draws = jax.random.uniform(jax.random.fold_in(jax.random.fold_in(stream_key, 6), dim), (shards_of,), jnp.float32, smallest / len(pieces), top_value / len(pieces))
        return jnp.repeat(jnp.exp(draws), shape[dim] // shards_of).reshape((-1,) + (1,) * (len(shape) - dim - 1))

    gain = one(*pieces[0])
    for cut in pieces[1:]:
        gain = gain * one(*cut)
    return gain


def gaussian(key, shape, width, reach, cuts=(), kind=jnp.bfloat16):
    entries = jax.random.normal(key, shape, jnp.float32) * width
    if len(cuts) > 0:
        entries = block_scale(key, shape, cuts, -0.22, 0.18) * entries
    return jnp.clip(entries, min=-reach, max=reach).astype(kind)


def setup_inputs(seed: int = 0, part: int = 0) -> dict:
    key_list = jax.random.split(jax.random.key(seed), 9)
    part_splits = jax.random.split(jax.random.fold_in(key_list[8], part), 9)
    return {
        "hidden": gaussian(part_splits[0], (SEQS, 2, D), 1.0, 6.0, ((0, 16),)),
        "wq": gaussian(key_list[1], (D, QUERY_HEADS * HEAD_SIZE), D ** -0.5, 0.0625, ((1, 8),)),
        "wkv": gaussian(key_list[2], (D, KEY_VALUE_WIDTH), D ** -0.5, 0.0625, ((1, 8),)),
        "cache_pool": draw_cache_pool(jax.random.fold_in(jax.random.fold_in(key_list[8], part), 71), part),
        "page_table": draw_page_table(jax.random.fold_in(jax.random.fold_in(key_list[8], part), 71), part),
        "ctx_len": touch_ends(jax.random.randint(part_splits[5], (SEQS,), 1, SEQ_PAGES * PAGE + 1), jax.random.fold_in(part_splits[5], 1), 1, SEQ_PAGES * PAGE).astype(jnp.int32),
        "prompt_slot": touch_ends(jax.random.randint(part_splits[6], (PROMPTS,), 0, SEQ_DEV), jax.random.fold_in(part_splits[6], 1), 0, SEQ_DEV - 1).astype(jnp.int32),
        "prompt_kv": gaussian(part_splits[7], (PROMPTS, PLEN, KEY_VALUE_WIDTH), 1.0, 6.0, ((0, 2), (2, 8))),
    }


def attend_block(query_rows, kv_new, prompt, pool, table, lens, slot):
    token_count = query_rows.shape[0]
    span = SEQ_PAGES * PAGE
    context = pool[table].reshape(token_count, span, KEY_VALUE_WIDTH)
    prompt_rows = jnp.broadcast_to(prompt[None], (token_count, PLEN, KEY_VALUE_WIDTH))
    combined_keys = jnp.concatenate([context, prompt_rows, kv_new], axis=1)
    valid_length = combined_keys.shape[1]
    where_key = jnp.arange(valid_length, dtype=jnp.int32)
    seq_local = jnp.arange(token_count, dtype=jnp.int32)
    step_ids = jnp.arange(2, dtype=jnp.int32)
    in_context = (where_key < span)[None, None, :]
    in_prompt = ((where_key >= span) & (where_key < span + PLEN))[None, None, :]
    context_ok = (where_key[None, :] < lens[:, None])[:, None, :]
    prompt_ok = (seq_local == slot)[:, None, None]
    new_ok = ((where_key - span - PLEN)[None, None, :] <= step_ids[None, :, None])
    live = jnp.where(in_context, context_ok, jnp.where(in_prompt, prompt_ok, new_ok))
    key_rows = combined_keys[:, :, :KEY_VALUE_HEADS * HEAD_SIZE].reshape(token_count, valid_length, KEY_VALUE_HEADS, HEAD_SIZE).astype(jnp.float32)
    value_rows = combined_keys[:, :, KEY_VALUE_HEADS * HEAD_SIZE:].reshape(token_count, valid_length, KEY_VALUE_HEADS, HEAD_SIZE).astype(jnp.float32)
    head_group = query_rows.reshape(token_count, 2, KEY_VALUE_HEADS, QUERY_HEADS // KEY_VALUE_HEADS, HEAD_SIZE).astype(jnp.float32)
    scores = jnp.einsum('sikgd,slkd->sikgl', head_group, key_rows) * (HEAD_SIZE ** -0.5)
    scores = jnp.where(live[:, :, None, None, :], scores, -1e30)
    top = jnp.max(scores, axis=-1, keepdims=True)
    expo = jnp.exp(scores - top)
    weights = (expo / jnp.sum(expo, axis=-1, keepdims=True)).astype(jnp.bfloat16)
    result = jnp.einsum('sikgl,slkd->sikgd', weights.astype(jnp.float32), value_rows)
    return result.astype(jnp.bfloat16).reshape(token_count, 2, QUERY_HEADS * HEAD_SIZE)


def reference(hidden, wq, wkv, cache_pool, page_table, ctx_len, prompt_slot, prompt_kv):
    blocks = N_TENSOR * N_BATCH
    flat = hidden.reshape(SEQS * 2, D)
    query_rows = jnp.dot(flat, wq, preferred_element_type=jnp.float32).astype(jnp.bfloat16)
    kv_new = jnp.dot(flat, wkv, preferred_element_type=jnp.float32).astype(jnp.bfloat16)
    query_rows = query_rows.reshape(blocks, SEQ_DEV, 2, QUERY_HEADS * HEAD_SIZE)
    kv_new = kv_new.reshape(blocks, SEQ_DEV, 2, KEY_VALUE_WIDTH)
    block_ids = jnp.arange(blocks, dtype=jnp.int32)
    owner = (block_ids % N_BATCH) * N_TENSOR + block_ids // N_BATCH
    prompts = prompt_kv[owner.astype(jnp.int32)]
    pools = cache_pool.reshape(blocks, POOL_DEV, PAGE, KEY_VALUE_WIDTH)
    tables = page_table.reshape(blocks, SEQ_DEV, SEQ_PAGES)
    lengths = ctx_len.reshape(blocks, SEQ_DEV)

    def one_block(items):
        return attend_block(*items)

    result = lax.map(one_block, (query_rows, kv_new, prompts, pools, tables, lengths, prompt_slot))
    return result.reshape(SEQS, 2, QUERY_HEADS * HEAD_SIZE)
```

```python
import functools

import jax
import jax.numpy as jnp
from jax import lax
from jax.experimental import pallas as pl
from jax.experimental.pallas import tpu as pltpu
from jax.sharding import PartitionSpec as P

QUERY_HEADS = 64
KEY_VALUE_HEADS = 8
HEAD_SIZE = 128
GROUP = QUERY_HEADS // KEY_VALUE_HEADS
STEPS = 2
MASKED = -1e30


def attend_kernel(
    table_ref, lens_ref, slot_ref, q_ref, kv_ref, prompt_ref, pool_ref, out_ref,
    pages, q_all, acc, top_all, sum_all, q_f32, sems, *, seqs, q_width, kv_off, kv_width, prompt_width,
):
    span_pages = table_ref.shape[0] // seqs
    page_rows = pool_ref.shape[1]
    span = span_pages * page_rows
    rows = STEPS * GROUP
    all_rows = KEY_VALUE_HEADS * rows
    value_at = KEY_VALUE_HEADS * HEAD_SIZE

    def page_copy(s, p):
        return pltpu.make_async_copy(
            pool_ref.at[table_ref[s * span_pages + p]],
            pages.at[s, pl.ds(p * page_rows, page_rows)],
            sems.at[s, p],
        )

    for s in range(seqs):
        for p in range(span_pages):
            page_copy(s, p).start()

    for h in range(QUERY_HEADS):
        k, g = h // GROUP, h % GROUP
        block, at = (h * HEAD_SIZE) // q_width, (h * HEAD_SIZE) % q_width
        q_f32[k, pl.ds(g, seqs * STEPS, stride=GROUP), :] = q_ref[block, :, at : at + HEAD_SIZE].astype(jnp.float32)
    q_all[...] = q_f32[...].astype(jnp.bfloat16)

    def new_tile(col):
        block, at = col // kv_width, kv_off + col % kv_width
        return kv_ref[block, :, at : at + HEAD_SIZE]

    def prompt_tile(col):
        block, at = col // prompt_width, col % prompt_width
        return prompt_ref[block, :, at : at + HEAD_SIZE]

    def scaled(q, keys):
        return lax.dot_general(
            q, keys, (((1,), (1,)), ((), ())), preferred_element_type=jnp.float32
        ) * HEAD_SIZE ** (-0.5)

    def mix(w, values):
        return jnp.dot(w.astype(jnp.bfloat16), values, preferred_element_type=jnp.float32)

    where_key = lax.broadcasted_iota(jnp.int32, (all_rows, span), 1)
    step_of = (lax.broadcasted_iota(jnp.int32, (all_rows, seqs * STEPS), 0) // GROUP) % STEPS
    new_at = lax.broadcasted_iota(jnp.int32, (all_rows, seqs * STEPS), 1)

    def one_sequence(s, carry):
        for p in range(span_pages):
            page_copy(s, p).wait()
        at = pl.multiple_of(s * rows, rows)
        q_s = [q_all[k, pl.ds(at, rows), :] for k in range(KEY_VALUE_HEADS)]
        sc = jnp.concatenate(
            [scaled(q_s[k], pages[s, :, k * HEAD_SIZE : (k + 1) * HEAD_SIZE]) for k in range(KEY_VALUE_HEADS)]
        )
        sn = jnp.concatenate([scaled(q_s[k], new_tile(k * HEAD_SIZE)) for k in range(KEY_VALUE_HEADS)])
        sc = jnp.where(where_key < lens_ref[s], sc, MASKED)
        offset = new_at - s * STEPS
        sn = jnp.where((offset >= 0) & (offset <= step_of), sn, MASKED)
        top = jnp.maximum(jnp.max(sc, axis=1, keepdims=True), jnp.max(sn, axis=1, keepdims=True))
        ec = jnp.exp(sc - top)
        en = jnp.exp(sn - top)
        total = jnp.sum(ec, axis=1, keepdims=True) + jnp.sum(en, axis=1, keepdims=True)
        for k in range(KEY_VALUE_HEADS):
            part = slice(k * rows, (k + 1) * rows)
            col = value_at + k * HEAD_SIZE
            acc[k, pl.ds(at, rows), :] = mix(ec[part], pages[s, :, col : col + HEAD_SIZE]) + mix(
                en[part], new_tile(col)
            )
            top_all[k, pl.ds(at, rows), :] = jnp.broadcast_to(top[part], (rows, HEAD_SIZE))
            sum_all[k, pl.ds(at, rows), :] = jnp.broadcast_to(total[part], (rows, HEAD_SIZE))
        return carry

    lax.fori_loop(0, seqs, one_sequence, 0, unroll=False)

    at = pl.multiple_of(slot_ref[0] * rows, rows)
    for k in range(KEY_VALUE_HEADS):
        mine = (k, pl.ds(at, rows), slice(None))
        sp = scaled(q_all[mine], prompt_tile(k * HEAD_SIZE))
        before = top_all[mine]
        top = jnp.maximum(before, jnp.max(sp, axis=1, keepdims=True))
        ep = jnp.exp(sp - top[:, :1])
        keep = jnp.exp(before - top)
        sum_all[mine] = sum_all[mine] * keep + jnp.sum(ep, axis=1, keepdims=True)
        acc[mine] = acc[mine] * keep + mix(ep, prompt_tile(value_at + k * HEAD_SIZE))

    acc[...] = acc[...] / sum_all[...]
    for h in range(QUERY_HEADS):
        k, g = h // GROUP, h % GROUP
        out_ref[:, h * HEAD_SIZE : (h + 1) * HEAD_SIZE] = acc[
            k, pl.ds(g, seqs * STEPS, stride=GROUP), :
        ].astype(jnp.bfloat16)


def attend(joined, q_width, prompt, pool, table, lens, slot):
    blocks, tokens, width = joined.shape
    seqs = tokens // STEPS
    kv_width = width - q_width
    kv_off = q_width
    kv = joined
    if kv_width % HEAD_SIZE:
        kv = joined[:, :, q_width:].transpose(1, 0, 2).reshape(1, tokens, blocks * kv_width)
        prompt = prompt.transpose(1, 0, 2).reshape(1, prompt.shape[1], blocks * kv_width)
        kv_width, kv_off = blocks * kv_width, 0
    rows = seqs * STEPS * GROUP
    span = table.shape[1] * pool.shape[1]
    smem = pl.BlockSpec(memory_space=pltpu.SMEM)
    vmem = pl.BlockSpec(memory_space=pltpu.VMEM)
    kernel = functools.partial(
        attend_kernel, seqs=seqs, q_width=q_width, kv_off=kv_off, kv_width=kv_width, prompt_width=prompt.shape[2]
    )
    big = pltpu.VMEM((KEY_VALUE_HEADS, rows, HEAD_SIZE), jnp.float32)
    return pl.pallas_call(
        kernel,
        out_shape=jax.ShapeDtypeStruct((tokens, QUERY_HEADS * HEAD_SIZE), jnp.bfloat16),
        in_specs=[smem, smem, smem, vmem, vmem, vmem, pl.BlockSpec(memory_space=pl.ANY)],
        out_specs=vmem,
        scratch_shapes=[
            pltpu.VMEM((seqs, span, pool.shape[2]), jnp.bfloat16),
            pltpu.VMEM((KEY_VALUE_HEADS, rows, HEAD_SIZE), jnp.bfloat16),
            big, big, big, big,
            pltpu.SemaphoreType.DMA((seqs, table.shape[1])),
        ],
        compiler_params=pltpu.CompilerParams(vmem_limit_bytes=24 << 20),
        name="attend",
    )(table.reshape(-1), lens, slot, joined, kv, prompt, pool)


def gather_blocks(own, axis, size):
    me = lax.axis_index(axis)
    line = size // 2
    place, side = me // 2, me % 2

    def hop(x, step, first, last):
        return lax.ppermute(
            x, axis, [(2 * c + p, 2 * (c + step) + p) for c in range(first, last + 1) for p in (0, 1)]
        )

    def swap(x, first, last):
        return lax.ppermute(x, axis, [(2 * c + p, 2 * c + 1 - p) for c in range(first, last + 1) for p in (0, 1)])

    up, down = {0: own}, {0: own}
    up_pair, down_pair = {}, {}
    found = [(own, me), (swap(own, 0, line - 1), 2 * place + 1 - side)]
    for s in range(1, line):
        up[s] = hop(up[s - 1], 1, s - 1, line - 2)
        down[s] = hop(down[s - 1], -1, 1, line - s)
        up_pair[s] = swap(up[s], s, line - 1)
        down_pair[s] = swap(down[s], 0, line - 1 - s)
    for s in range(1, line):
        other = (place + line - s) % line
        first = place >= s
        found.append((jnp.where(first, up[s], down[line - s]), 2 * other + side))
        found.append((jnp.where(first, up_pair[s], down_pair[line - s]), 2 * other + 1 - side))
    return found


def per_device(size, hidden, wq, wkv, cache_pool, page_table, ctx_len, prompt_slot, prompt_kv):
    tokens = hidden.shape[0] * hidden.shape[1]
    own = hidden.reshape(tokens, hidden.shape[2])
    found = gather_blocks(own, "tensor", size)
    rows = jnp.concatenate([b for b, _ in found])
    prompt = lax.all_to_all(prompt_kv, "tensor", split_axis=0, concat_axis=0, tiled=True)
    query = jnp.dot(rows, wq, preferred_element_type=jnp.float32).astype(jnp.bfloat16)
    keyval = jnp.dot(rows, wkv, preferred_element_type=jnp.float32).astype(jnp.bfloat16)
    joined = jnp.concatenate([query, keyval], axis=1).reshape(size, tokens, -1)
    ordered = joined
    for j, (_, owner) in enumerate(found):
        ordered = lax.dynamic_update_slice(ordered, joined[j][None], (owner, 0, 0))
    back = lax.all_to_all(ordered, "tensor", split_axis=0, concat_axis=0, tiled=True)
    out = attend(back, wq.shape[1], prompt, cache_pool, page_table, ctx_len, prompt_slot)
    return out.reshape(hidden.shape[0], hidden.shape[1], -1)


def solution(mesh):
    placed = (
        P(("groups", "tensor", "batch"), None, None),
        P(None, "tensor"),
        P(None, "tensor"),
        P(("groups", "tensor", "batch"), None, None),
        P(("groups", "tensor", "batch"), None),
        P(("groups", "tensor", "batch")),
        P(("groups", "tensor", "batch")),
        P(("groups", "batch"), None, "tensor"),
    )
    return jax.shard_map(
        functools.partial(per_device, mesh.shape["tensor"]),
        mesh=mesh,
        in_specs=placed,
        out_specs=P(("groups", "tensor", "batch"), None, None),
        check_vma=False,
    )
```

```python
import functools

import jax
import jax.numpy as jnp
from jax import lax
from jax.experimental import pallas as pl
from jax.experimental.pallas import tpu as pltpu
from jax.sharding import PartitionSpec as P


QUERY_HEADS = 64
KEY_VALUE_HEADS = 8
HEAD_SIZE = 128
GROUP = QUERY_HEADS // KEY_VALUE_HEADS
STEPS = 2
MASKED = -1e30
LOAD_LIMIT = 34 << 20
ATTEND_LIMIT = 52 << 20


def attend_kernel(
    table_ref, lens_ref, slot_ref, q_ref, kv_ref, prompt_ref, pool_ref, out_ref,
    pages, q_all, acc, top_all, sum_all, q_f32, sems, *, seqs, q_width, kv_off, kv_width, prompt_width,
):
    span_pages = table_ref.shape[0] // seqs
    page_rows = pool_ref.shape[1]
    span = span_pages * page_rows
    rows = STEPS * GROUP
    all_rows = KEY_VALUE_HEADS * rows
    value_at = KEY_VALUE_HEADS * HEAD_SIZE

    def page_copy(s, p):
        return pltpu.make_async_copy(
            pool_ref.at[table_ref[s * span_pages + p]],
            pages.at[s, pl.ds(p * page_rows, page_rows)],
            sems.at[s, p],
        )

    for s in range(seqs):
        for p in range(span_pages):
            page_copy(s, p).start()

    for h in range(QUERY_HEADS):
        k, g = h // GROUP, h % GROUP
        block, at = (h * HEAD_SIZE) // q_width, (h * HEAD_SIZE) % q_width
        q_f32[k, pl.ds(g, seqs * STEPS, stride=GROUP), :] = q_ref[block, :, at : at + HEAD_SIZE].astype(jnp.float32)
    q_all[...] = q_f32[...].astype(jnp.bfloat16)

    def new_tile(col):
        block, at = col // kv_width, kv_off + col % kv_width
        return kv_ref[block, :, at : at + HEAD_SIZE]

    def prompt_tile(col):
        block, at = col // prompt_width, col % prompt_width
        return prompt_ref[block, :, at : at + HEAD_SIZE]

    def scaled(q, keys):
        return lax.dot_general(
            q, keys, (((1,), (1,)), ((), ())), preferred_element_type=jnp.float32
        ) * HEAD_SIZE ** (-0.5)

    def mix(w, values):
        return jnp.dot(w.astype(jnp.bfloat16), values, preferred_element_type=jnp.float32)

    where_key = lax.broadcasted_iota(jnp.int32, (all_rows, span), 1)
    step_of = (lax.broadcasted_iota(jnp.int32, (all_rows, seqs * STEPS), 0) // GROUP) % STEPS
    new_at = lax.broadcasted_iota(jnp.int32, (all_rows, seqs * STEPS), 1)

    def one_sequence(s, carry):
        for p in range(span_pages):
            page_copy(s, p).wait()

        def cached(col):
            return pages[s, :, col : col + HEAD_SIZE]

        at = pl.multiple_of(s * rows, rows)
        q_s = [q_all[k, pl.ds(at, rows), :] for k in range(KEY_VALUE_HEADS)]
        sc = jnp.concatenate(
            [scaled(q_s[k], cached(k * HEAD_SIZE)) for k in range(KEY_VALUE_HEADS)]
        )
        sn = jnp.concatenate([scaled(q_s[k], new_tile(k * HEAD_SIZE)) for k in range(KEY_VALUE_HEADS)])
        sc = jnp.where(where_key < lens_ref[s], sc, MASKED)
        offset = new_at - s * STEPS
        sn = jnp.where((offset >= 0) & (offset <= step_of), sn, MASKED)
        top = jnp.maximum(jnp.max(sc, axis=1, keepdims=True), jnp.max(sn, axis=1, keepdims=True))
        ec = jnp.exp(sc - top)
        en = jnp.exp(sn - top)
        total = jnp.sum(ec, axis=1, keepdims=True) + jnp.sum(en, axis=1, keepdims=True)
        for k in range(KEY_VALUE_HEADS):
            part = slice(k * rows, (k + 1) * rows)
            col = value_at + k * HEAD_SIZE
            acc[k, pl.ds(at, rows), :] = mix(ec[part], cached(col)) + mix(
                en[part], new_tile(col)
            )
            top_all[k, pl.ds(at, rows), :] = jnp.broadcast_to(top[part], (rows, HEAD_SIZE))
            sum_all[k, pl.ds(at, rows), :] = jnp.broadcast_to(total[part], (rows, HEAD_SIZE))
        return carry

    lax.fori_loop(0, seqs, one_sequence, 0, unroll=False)

    at = pl.multiple_of(slot_ref[0] * rows, rows)
    for k in range(KEY_VALUE_HEADS):
        mine = (k, pl.ds(at, rows), slice(None))
        sp = scaled(q_all[mine], prompt_tile(k * HEAD_SIZE))
        before = top_all[mine]
        top = jnp.maximum(before, jnp.max(sp, axis=1, keepdims=True))
        ep = jnp.exp(sp - top[:, :1])
        keep = jnp.exp(before - top)
        sum_all[mine] = sum_all[mine] * keep + jnp.sum(ep, axis=1, keepdims=True)
        acc[mine] = acc[mine] * keep + mix(ep, prompt_tile(value_at + k * HEAD_SIZE))

    acc[...] = acc[...] / sum_all[...]
    for h in range(QUERY_HEADS):
        k, g = h // GROUP, h % GROUP
        out_ref[:, h * HEAD_SIZE : (h + 1) * HEAD_SIZE] = acc[
            k, pl.ds(g, seqs * STEPS, stride=GROUP), :
        ].astype(jnp.bfloat16)


def attend(joined, q_width, prompt, pool, table, lens, slot):
    blocks, tokens, width = joined.shape
    seqs = tokens // STEPS
    kv_width = width - q_width
    kv_off = q_width
    kv = joined
    if kv_width % HEAD_SIZE:
        kv = joined[:, :, q_width:].transpose(1, 0, 2).reshape(1, tokens, blocks * kv_width)
        prompt = prompt.transpose(1, 0, 2).reshape(1, prompt.shape[1], blocks * kv_width)
        kv_width, kv_off = blocks * kv_width, 0
    rows = seqs * STEPS * GROUP
    smem = pl.BlockSpec(memory_space=pltpu.SMEM)
    vmem = pl.BlockSpec(memory_space=pltpu.VMEM)
    kernel = functools.partial(
        attend_kernel, seqs=seqs, q_width=q_width, kv_off=kv_off, kv_width=kv_width, prompt_width=prompt.shape[2]
    )
    big = pltpu.VMEM((KEY_VALUE_HEADS, rows, HEAD_SIZE), jnp.float32)
    return pl.pallas_call(
        kernel,
        out_shape=jax.ShapeDtypeStruct((tokens, QUERY_HEADS * HEAD_SIZE), jnp.bfloat16),
        in_specs=[smem, smem, smem, vmem, vmem, vmem, pl.BlockSpec(memory_space=pl.ANY)],
        out_specs=vmem,
        scratch_shapes=[
            pltpu.VMEM((seqs, table.shape[1] * pool.shape[1], pool.shape[2]), jnp.bfloat16),
            pltpu.VMEM((KEY_VALUE_HEADS, rows, HEAD_SIZE), jnp.bfloat16),
            big, big, big, big,
            pltpu.SemaphoreType.DMA((seqs, table.shape[1])),
        ],
        compiler_params=pltpu.CompilerParams(vmem_limit_bytes=ATTEND_LIMIT),
        name="attend",
    )(table.reshape(-1), lens, slot, joined, kv, prompt, pool)


def gather_blocks(own, axis, size):
    me = lax.axis_index(axis)
    line = size // 2
    place, side = me // 2, me % 2

    def hop(x, step, first, last):
        return lax.ppermute(
            x, axis, [(2 * c + p, 2 * (c + step) + p) for c in range(first, last + 1) for p in (0, 1)]
        )

    def swap(x, first, last):
        return lax.ppermute(x, axis, [(2 * c + p, 2 * c + 1 - p) for c in range(first, last + 1) for p in (0, 1)])

    up, down = {0: own}, {0: own}
    up_pair, down_pair = {}, {}
    found = [(own, me), (swap(own, 0, line - 1), 2 * place + 1 - side)]
    for s in range(1, line):
        up[s] = hop(up[s - 1], 1, s - 1, line - 2)
        down[s] = hop(down[s - 1], -1, 1, line - s)
        up_pair[s] = swap(up[s], s, line - 1)
        down_pair[s] = swap(down[s], 0, line - 1 - s)
    for s in range(1, line):
        other = (place + line - s) % line
        first = place >= s
        found.append((jnp.where(first, up[s], down[line - s]), 2 * other + side))
        found.append((jnp.where(first, up_pair[s], down_pair[line - s]), 2 * other + 1 - side))
    return found, (up[line - 1], down[line - 1])


def project_kernel(owner_ref, x_ref, w_ref, out_ref, *, tile):
    blocks, tokens, width = out_ref.shape

    def one_tile(i, carry):
        cols = pl.ds(pl.multiple_of(i * tile, tile), tile)
        y = jnp.dot(x_ref[...], w_ref[:, cols], preferred_element_type=jnp.float32).astype(jnp.bfloat16)
        for j in range(blocks):
            out_ref[owner_ref[j], :, cols] = y[j * tokens : (j + 1) * tokens]
        return carry

    lax.fori_loop(0, width // tile, one_tile, 0)


def project(owners, rows, weights):
    blocks = owners.shape[0]
    tokens = rows.shape[0] // blocks
    width = weights.shape[1]
    tile = next(t for t in (2 * HEAD_SIZE, HEAD_SIZE, width) if width % t == 0)
    smem = pl.BlockSpec(memory_space=pltpu.SMEM)
    vmem = pl.BlockSpec(memory_space=pltpu.VMEM)
    return pl.pallas_call(
        functools.partial(project_kernel, tile=tile),
        out_shape=jax.ShapeDtypeStruct((blocks, tokens, width), jnp.bfloat16),
        in_specs=[smem, vmem, vmem],
        out_specs=vmem,
        compiler_params=pltpu.CompilerParams(vmem_limit_bytes=6 << 20),
        cost_estimate=pl.CostEstimate(flops=2 * rows.size * width, bytes_accessed=2 * rows.size, transcendentals=0),
        name="project",
    )(owners, rows, weights)


def load_kernel(token_ref, wq_ref, wkv_ref, out_ref, sems, *, parts):
    depth = wq_ref.shape[0] // parts
    q_width, kv_width = wq_ref.shape[1], wkv_ref.shape[1]
    copies = []
    for i in range(parts):
        rows = pl.ds(i * depth, depth)
        copies.append(pltpu.make_async_copy(wq_ref.at[rows], out_ref.at[rows, pl.ds(0, q_width)], sems.at[0, i]))
    copies.append(pltpu.make_async_copy(wkv_ref, out_ref.at[:, pl.ds(q_width, kv_width)], sems.at[1, 0]))
    for c in copies:
        c.start()
    for c in copies:
        c.wait()


def load(token, wq, wkv):
    parts = 4
    hbm = pl.BlockSpec(memory_space=pl.ANY)
    shape = (wq.shape[0], wq.shape[1] + wkv.shape[1])
    return pl.pallas_call(
        functools.partial(load_kernel, parts=parts),
        out_shape=pltpu.VMEM(shape, wq.dtype),
        in_specs=[hbm, hbm, hbm],
        out_specs=pl.BlockSpec(memory_space=pltpu.VMEM),
        scratch_shapes=[pltpu.SemaphoreType.DMA((2, parts))],
        compiler_params=pltpu.CompilerParams(vmem_limit_bytes=LOAD_LIMIT),
        cost_estimate=pl.CostEstimate(flops=0, bytes_accessed=2 * shape[0] * shape[1], transcendentals=0),
        name="load",
    )(token, wq, wkv)


def per_device(size, hidden, wq, wkv, cache_pool, page_table, ctx_len, prompt_slot, prompt_kv):
    tokens = hidden.shape[0] * hidden.shape[1]
    own = hidden.reshape(tokens, hidden.shape[2])
    found, late = gather_blocks(own, "tensor", size)
    rows = jnp.concatenate([b for b, _ in found])
    owners = jnp.stack([o for _, o in found]).astype(jnp.int32)
    prompt_kv, _ = lax.optimization_barrier((prompt_kv, late))
    prompt = lax.all_to_all(prompt_kv, "tensor", split_axis=0, concat_axis=0, tiled=True)
    weights = load(late[0][:8, :HEAD_SIZE], wq, wkv)
    joined = project(owners, rows, weights)
    joined, prompt = lax.optimization_barrier((joined, prompt))
    back = lax.all_to_all(joined, "tensor", split_axis=0, concat_axis=0, tiled=True)
    out = attend(back, wq.shape[1], prompt, cache_pool, page_table, ctx_len, prompt_slot)
    return out.reshape(hidden.shape[0], hidden.shape[1], -1)


def solution(mesh):
    placed = (
        P(("groups", "tensor", "batch"), None, None),
        P(None, "tensor"),
        P(None, "tensor"),
        P(("groups", "tensor", "batch"), None, None),
        P(("groups", "tensor", "batch"), None),
        P(("groups", "tensor", "batch")),
        P(("groups", "tensor", "batch")),
        P(("groups", "batch"), None, "tensor"),
    )
    return jax.shard_map(
        functools.partial(per_device, mesh.shape["tensor"]),
        mesh=mesh,
        in_specs=placed,
        out_specs=P(("groups", "tensor", "batch"), None, None),
        check_vma=False,
    )
```

```python
import functools

import jax
import jax.numpy as jnp
from jax import lax
from jax.experimental import pallas as pl
from jax.experimental.pallas import tpu as pltpu
from jax.sharding import PartitionSpec as P


QUERY_HEADS = 64
KEY_VALUE_HEADS = 8
HEAD_SIZE = 128
GROUP = QUERY_HEADS // KEY_VALUE_HEADS
STEPS = 2
MASKED = -1e30
PROJECT_LIMIT = 48 << 20
ATTEND_LIMIT = 52 << 20


def attend_kernel(
    table_ref, lens_ref, slot_ref, q_ref, kv_ref, prompt_ref, pool_ref, out_ref,
    pages, q_all, acc, top_all, sum_all, q_f32, sems, *, seqs, q_width, kv_off, kv_width, prompt_width,
):
    span_pages = table_ref.shape[0] // seqs
    page_rows = pool_ref.shape[1]
    span = span_pages * page_rows
    rows = STEPS * GROUP
    all_rows = KEY_VALUE_HEADS * rows
    value_at = KEY_VALUE_HEADS * HEAD_SIZE

    def page_copy(s, p):
        return pltpu.make_async_copy(
            pool_ref.at[table_ref[s * span_pages + p]],
            pages.at[s, pl.ds(p * page_rows, page_rows)],
            sems.at[s, p],
        )

    for s in range(seqs):
        for p in range(span_pages):
            page_copy(s, p).start()

    for h in range(QUERY_HEADS):
        k, g = h // GROUP, h % GROUP
        block, at = (h * HEAD_SIZE) // q_width, (h * HEAD_SIZE) % q_width
        q_f32[k, pl.ds(g, seqs * STEPS, stride=GROUP), :] = q_ref[block, :, at : at + HEAD_SIZE].astype(jnp.float32)
    q_all[...] = q_f32[...].astype(jnp.bfloat16)

    def new_tile(col):
        block, at = col // kv_width, kv_off + col % kv_width
        return kv_ref[block, :, at : at + HEAD_SIZE]

    def prompt_tile(col):
        block, at = col // prompt_width, col % prompt_width
        return prompt_ref[block, :, at : at + HEAD_SIZE]

    def scaled(q, keys):
        return lax.dot_general(
            q, keys, (((1,), (1,)), ((), ())), preferred_element_type=jnp.float32
        ) * HEAD_SIZE ** (-0.5)

    def mix(w, values):
        return jnp.dot(w.astype(jnp.bfloat16), values, preferred_element_type=jnp.float32)

    where_key = lax.broadcasted_iota(jnp.int32, (all_rows, span), 1)
    step_of = (lax.broadcasted_iota(jnp.int32, (all_rows, seqs * STEPS), 0) // GROUP) % STEPS
    new_at = lax.broadcasted_iota(jnp.int32, (all_rows, seqs * STEPS), 1)

    def one_sequence(s, carry):
        for p in range(span_pages):
            page_copy(s, p).wait()

        def cached(col):
            return pages[s, :, col : col + HEAD_SIZE]

        at = pl.multiple_of(s * rows, rows)
        q_s = [q_all[k, pl.ds(at, rows), :] for k in range(KEY_VALUE_HEADS)]
        sc = jnp.concatenate(
            [scaled(q_s[k], cached(k * HEAD_SIZE)) for k in range(KEY_VALUE_HEADS)]
        )
        sn = jnp.concatenate([scaled(q_s[k], new_tile(k * HEAD_SIZE)) for k in range(KEY_VALUE_HEADS)])
        sc = jnp.where(where_key < lens_ref[s], sc, MASKED)
        offset = new_at - s * STEPS
        sn = jnp.where((offset >= 0) & (offset <= step_of), sn, MASKED)
        top = jnp.maximum(jnp.max(sc, axis=1, keepdims=True), jnp.max(sn, axis=1, keepdims=True))
        ec = jnp.exp(sc - top)
        en = jnp.exp(sn - top)
        total = jnp.sum(ec, axis=1, keepdims=True) + jnp.sum(en, axis=1, keepdims=True)
        for k in range(KEY_VALUE_HEADS):
            part = slice(k * rows, (k + 1) * rows)
            col = value_at + k * HEAD_SIZE
            acc[k, pl.ds(at, rows), :] = mix(ec[part], cached(col)) + mix(
                en[part], new_tile(col)
            )
            top_all[k, pl.ds(at, rows), :] = jnp.broadcast_to(top[part], (rows, HEAD_SIZE))
            sum_all[k, pl.ds(at, rows), :] = jnp.broadcast_to(total[part], (rows, HEAD_SIZE))
        return carry

    lax.fori_loop(0, seqs, one_sequence, 0, unroll=False)

    at = pl.multiple_of(slot_ref[0] * rows, rows)
    for k in range(KEY_VALUE_HEADS):
        mine = (k, pl.ds(at, rows), slice(None))
        sp = scaled(q_all[mine], prompt_tile(k * HEAD_SIZE))
        before = top_all[mine]
        top = jnp.maximum(before, jnp.max(sp, axis=1, keepdims=True))
        ep = jnp.exp(sp - top[:, :1])
        keep = jnp.exp(before - top)
        sum_all[mine] = sum_all[mine] * keep + jnp.sum(ep, axis=1, keepdims=True)
        acc[mine] = acc[mine] * keep + mix(ep, prompt_tile(value_at + k * HEAD_SIZE))

    acc[...] = acc[...] / sum_all[...]
    for h in range(QUERY_HEADS):
        k, g = h // GROUP, h % GROUP
        out_ref[:, h * HEAD_SIZE : (h + 1) * HEAD_SIZE] = acc[
            k, pl.ds(g, seqs * STEPS, stride=GROUP), :
        ].astype(jnp.bfloat16)


def attend(joined, q_width, prompt, pool, table, lens, slot):
    blocks, tokens, width = joined.shape
    seqs = tokens // STEPS
    kv_width = width - q_width
    kv_off = q_width
    kv = joined
    if kv_width % HEAD_SIZE:
        kv = joined[:, :, q_width:].transpose(1, 0, 2).reshape(1, tokens, blocks * kv_width)
        prompt = prompt.transpose(1, 0, 2).reshape(1, prompt.shape[1], blocks * kv_width)
        kv_width, kv_off = blocks * kv_width, 0
    rows = seqs * STEPS * GROUP
    smem = pl.BlockSpec(memory_space=pltpu.SMEM)
    vmem = pl.BlockSpec(memory_space=pltpu.VMEM)
    kernel = functools.partial(
        attend_kernel, seqs=seqs, q_width=q_width, kv_off=kv_off, kv_width=kv_width, prompt_width=prompt.shape[2]
    )
    big = pltpu.VMEM((KEY_VALUE_HEADS, rows, HEAD_SIZE), jnp.float32)
    return pl.pallas_call(
        kernel,
        out_shape=jax.ShapeDtypeStruct((tokens, QUERY_HEADS * HEAD_SIZE), jnp.bfloat16),
        in_specs=[smem, smem, smem, vmem, vmem, vmem, pl.BlockSpec(memory_space=pl.ANY)],
        out_specs=vmem,
        scratch_shapes=[
            pltpu.VMEM((seqs, table.shape[1] * pool.shape[1], pool.shape[2]), jnp.bfloat16),
            pltpu.VMEM((KEY_VALUE_HEADS, rows, HEAD_SIZE), jnp.bfloat16),
            big, big, big, big,
            pltpu.SemaphoreType.DMA((seqs, table.shape[1])),
        ],
        compiler_params=pltpu.CompilerParams(vmem_limit_bytes=ATTEND_LIMIT),
        name="attend",
    )(table.reshape(-1), lens, slot, joined, kv, prompt, pool)


def gather_blocks(own, axis, size):
    me = lax.axis_index(axis)
    line = size // 2
    place, side = me // 2, me % 2

    def hop(x, step, first, last):
        return lax.ppermute(
            x, axis, [(2 * c + p, 2 * (c + step) + p) for c in range(first, last + 1) for p in (0, 1)]
        )

    def swap(x, first, last):
        return lax.ppermute(x, axis, [(2 * c + p, 2 * c + 1 - p) for c in range(first, last + 1) for p in (0, 1)])

    up, down = {0: own}, {0: own}
    up_pair, down_pair = {}, {}
    near = swap(own, 0, line - 1)
    found = [((own,), 0, me), ((near,), 0, 2 * place + 1 - side)]
    for s in range(1, line):
        up[s] = hop(up[s - 1], 1, s - 1, line - 2)
        down[s] = hop(down[s - 1], -1, 1, line - s)
        up_pair[s] = swap(up[s], s, line - 1)
        down_pair[s] = swap(down[s], 0, line - 1 - s)
    for s in range(1, line):
        other = (place + line - s) % line
        first = place >= s
        found.append(((up[s], down[line - s]), 1 - first.astype(jnp.int32), 2 * other + side))
        found.append(((up_pair[s], down_pair[line - s]), 1 - first.astype(jnp.int32), 2 * other + 1 - side))
    return found, (up[line - 1], down[line - 1])


def project_kernel(owner_ref, choice_ref, *refs, tiles, counts):
    blocks = sum(counts)
    sources = refs[:blocks]
    wq_ref, wkv_ref, out_ref, x_here, w_here, x_sems, w_sems = refs[blocks:]
    size, tokens, _ = out_ref.shape
    q_width = wq_ref.shape[1]

    def fetch(j, source):
        rows = pl.ds(pl.multiple_of(owner_ref[j] * tokens, tokens), tokens)
        return pltpu.make_async_copy(source, x_here.at[rows], x_sems.at[j])

    at = 0
    firsts = []
    for j, count in enumerate(counts):
        firsts.append(sources[at])
        if count == 1:
            fetch(j, sources[at]).start()
        else:
            one, other = sources[at], sources[at + 1]

            @pl.when(choice_ref[j] == 0)
            def _():
                fetch(j, one).start()

            @pl.when(choice_ref[j] != 0)
            def _():
                fetch(j, other).start()

        at += count
    copies = []
    for i, (at, width) in enumerate(tiles):
        source = wq_ref.at[:, pl.ds(at, width)] if at < q_width else wkv_ref.at[:, pl.ds(at - q_width, width)]
        copies.append(pltpu.make_async_copy(source, w_here.at[:, pl.ds(at, width)], w_sems.at[i]))
    for c in copies:
        c.start()
    for j, source in enumerate(firsts):
        fetch(j, source).wait()

    for c, (at, width) in zip(copies, tiles):
        c.wait()
        cols = slice(at, at + width)
        y = jnp.dot(x_here[...], w_here[:, cols], preferred_element_type=jnp.float32).astype(jnp.bfloat16)
        for j in range(size):
            out_ref[j, :, cols] = y[j * tokens : (j + 1) * tokens]


def project(found, wq, wkv):
    size = len(found)
    tokens = found[0][0][0].shape[0]
    depth, q_width = wq.shape
    width = q_width + wkv.shape[1]
    wide = 2 * HEAD_SIZE
    tiles = [(at, min(wide, q_width - at)) for at in range(0, q_width, wide)]
    tiles += [(at, min(HEAD_SIZE, width - at)) for at in range(q_width, width, HEAD_SIZE)]
    counts = [len(options) for options, _, _ in found]
    sources = [block for options, _, _ in found for block in options]
    choices = jnp.stack([jnp.asarray(choice, jnp.int32) for _, choice, _ in found])
    owners = jnp.stack([jnp.asarray(owner, jnp.int32) for _, _, owner in found])
    smem = pl.BlockSpec(memory_space=pltpu.SMEM)
    vmem = pl.BlockSpec(memory_space=pltpu.VMEM)
    hbm = pl.BlockSpec(memory_space=pl.ANY)
    return pl.pallas_call(
        functools.partial(project_kernel, tiles=tiles, counts=counts),
        out_shape=jax.ShapeDtypeStruct((size, tokens, width), jnp.bfloat16),
        in_specs=[smem, smem] + [hbm] * len(sources) + [hbm, hbm],
        out_specs=vmem,
        scratch_shapes=[
            pltpu.VMEM((size * tokens, depth), wq.dtype),
            pltpu.VMEM((depth, width), wq.dtype),
            pltpu.SemaphoreType.DMA((size,)),
            pltpu.SemaphoreType.DMA((len(tiles),)),
        ],
        compiler_params=pltpu.CompilerParams(vmem_limit_bytes=PROJECT_LIMIT),
        cost_estimate=pl.CostEstimate(
            flops=2 * size * tokens * depth * width,
            bytes_accessed=2 * depth * (size * tokens + width),
            transcendentals=0,
        ),
        name="project",
    )(owners, choices, *sources, wq, wkv)


def per_device(size, hidden, wq, wkv, cache_pool, page_table, ctx_len, prompt_slot, prompt_kv):
    tokens = hidden.shape[0] * hidden.shape[1]
    own = hidden.reshape(tokens, hidden.shape[2])
    found, late = gather_blocks(own, "tensor", size)
    prompt_kv, _ = lax.optimization_barrier((prompt_kv, late))
    prompt = lax.all_to_all(prompt_kv, "tensor", split_axis=0, concat_axis=0, tiled=True)
    joined = project(found, wq, wkv)
    joined, prompt = lax.optimization_barrier((joined, prompt))
    back = lax.all_to_all(joined, "tensor", split_axis=0, concat_axis=0, tiled=True)
    out = attend(back, wq.shape[1], prompt, cache_pool, page_table, ctx_len, prompt_slot)
    return out.reshape(hidden.shape[0], hidden.shape[1], -1)


def solution(mesh):
    placed = (
        P(("groups", "tensor", "batch"), None, None),
        P(None, "tensor"),
        P(None, "tensor"),
        P(("groups", "tensor", "batch"), None, None),
        P(("groups", "tensor", "batch"), None),
        P(("groups", "tensor", "batch")),
        P(("groups", "tensor", "batch")),
        P(("groups", "batch"), None, "tensor"),
    )
    return jax.shard_map(
        functools.partial(per_device, mesh.shape["tensor"]),
        mesh=mesh,
        in_specs=placed,
        out_specs=P(("groups", "tensor", "batch"), None, None),
        check_vma=False,
    )
```

```python
import functools

import jax
import jax.numpy as jnp
from jax import lax
from jax.experimental import pallas as pl
from jax.experimental.pallas import tpu as pltpu
from jax.sharding import PartitionSpec as P


QUERY_HEADS = 64
KEY_VALUE_HEADS = 8
HEAD_SIZE = 128
GROUP = QUERY_HEADS // KEY_VALUE_HEADS
STEPS = 2
MASKED = -1e30
PROJECT_LIMIT = 48 << 20
AHEAD = 2
PAGES_AHEAD = 3
UNROLL = 1
ATTEND_LIMIT = 52 << 20


def attend_kernel(
    table_ref, lens_ref, slot_ref, q_ref, kv_ref, prompt_ref, pool_ref, out_ref,
    pages, q_pairs, new_scores, new_weights, acc, top_all, sum_all, q_f32, sems,
    *, seqs, q_width, kv_off, kv_width, prompt_width,
):
    span_pages = table_ref.shape[0] // seqs
    page_rows = pool_ref.shape[1]
    span = span_pages * page_rows
    rows = STEPS * GROUP
    new_rows = seqs * STEPS
    all_rows = KEY_VALUE_HEADS * rows
    pairs = KEY_VALUE_HEADS // 2
    wide = 2 * HEAD_SIZE
    value_at = KEY_VALUE_HEADS * HEAD_SIZE
    heads = range(KEY_VALUE_HEADS)

    def page_copy(s, p):
        return pltpu.make_async_copy(
            pool_ref.at[table_ref[s * span_pages + p]],
            pages.at[s, pl.ds(p * page_rows, page_rows)],
            sems.at[s, p],
        )

    for s in range(min(PAGES_AHEAD, seqs)):
        for p in range(span_pages):
            page_copy(s, p).start()

    def new_pair(col):
        block, at = col // kv_width, kv_off + col % kv_width
        return kv_ref[block, :, at : at + wide]

    def prompt_pair(col):
        block, at = col // prompt_width, col % prompt_width
        return prompt_ref[block, :, at : at + wide]

    def scaled(q, keys):
        return lax.dot_general(
            q, keys, (((1,), (1,)), ((), ())), preferred_element_type=jnp.float32
        ) * HEAD_SIZE ** (-0.5)

    def mix(w, values):
        return jnp.dot(w.astype(jnp.bfloat16), values, preferred_element_type=jnp.float32)

    for h in range(QUERY_HEADS):
        k, g = h // GROUP, h % GROUP
        block, at = (h * HEAD_SIZE) // q_width, (h * HEAD_SIZE) % q_width
        q_f32[k, pl.ds(g, new_rows, stride=GROUP), :] = q_ref[block, :, at : at + HEAD_SIZE].astype(jnp.float32)
    blank = jnp.zeros((seqs, rows, HEAD_SIZE), jnp.bfloat16)
    for k in heads:
        j, half = k // 2, k % 2
        mine = slice(half * rows, (half + 1) * rows)
        q_pairs[j, :, mine, half * HEAD_SIZE : (half + 1) * HEAD_SIZE] = (
            q_f32[k].astype(jnp.bfloat16).reshape(seqs, rows, HEAD_SIZE)
        )
        q_pairs[j, :, mine, (1 - half) * HEAD_SIZE : (2 - half) * HEAD_SIZE] = blank

    step_of = (lax.broadcasted_iota(jnp.int32, (seqs, 2 * rows, new_rows), 1) // GROUP) % STEPS
    seq_of = lax.broadcasted_iota(jnp.int32, (seqs, 2 * rows, new_rows), 0)
    offset = lax.broadcasted_iota(jnp.int32, (seqs, 2 * rows, new_rows), 2) - seq_of * STEPS
    live_new = (offset >= 0) & (offset <= step_of)
    for j in range(pairs):
        sn = scaled(q_pairs[j].reshape(seqs * 2 * rows, wide), new_pair(j * wide))
        new_scores[:, j * 2 * rows : (j + 1) * 2 * rows, :] = jnp.where(
            live_new, sn.reshape(seqs, 2 * rows, new_rows), MASKED
        )

    where_key = lax.broadcasted_iota(jnp.int32, (all_rows, span), 1)

    def one_sequence(s, carry):
        @pl.when(s + PAGES_AHEAD < seqs)
        def _():
            for p in range(span_pages):
                page_copy(s + PAGES_AHEAD, p).start()

        for p in range(span_pages):
            page_copy(s, p).wait()

        at = pl.multiple_of(s * rows, rows)
        sc = jnp.concatenate(
            [scaled(q_pairs[j, s], pages[s, :, j * wide : (j + 1) * wide]) for j in range(pairs)]
        )
        sc = jnp.where(where_key < lens_ref[s], sc, MASKED)
        sn = new_scores[s]
        top = jnp.maximum(jnp.max(sc, axis=1, keepdims=True), jnp.max(sn, axis=1, keepdims=True))
        ec = jnp.exp(sc - top)
        en = jnp.exp(sn - top)
        total = jnp.sum(ec, axis=1, keepdims=True) + jnp.sum(en, axis=1, keepdims=True)
        new_weights[s] = en.astype(jnp.bfloat16)
        for j in range(pairs):
            col = value_at + j * wide
            both = mix(ec[j * 2 * rows : (j + 1) * 2 * rows], pages[s, :, col : col + wide])
            acc[2 * j, pl.ds(at, rows), :] = both[:rows, :HEAD_SIZE]
            acc[2 * j + 1, pl.ds(at, rows), :] = both[rows:, HEAD_SIZE:]
        for k in heads:
            part = slice(k * rows, (k + 1) * rows)
            top_all[k, pl.ds(at, rows), :] = jnp.broadcast_to(top[part], (rows, HEAD_SIZE))
            sum_all[k, pl.ds(at, rows), :] = jnp.broadcast_to(total[part], (rows, HEAD_SIZE))
        return carry

    lax.fori_loop(0, seqs, one_sequence, 0, unroll=UNROLL)

    for j in range(pairs):
        w = new_weights[:, j * 2 * rows : (j + 1) * 2 * rows, :].reshape(seqs * 2 * rows, new_rows)
        both = mix(w, new_pair(value_at + j * wide)).reshape(seqs, 2 * rows, wide)
        acc[2 * j] += both[:, :rows, :HEAD_SIZE].reshape(seqs * rows, HEAD_SIZE)
        acc[2 * j + 1] += both[:, rows:, HEAD_SIZE:].reshape(seqs * rows, HEAD_SIZE)

    slot = slot_ref[0]
    mine = pl.ds(pl.multiple_of(slot * rows, rows), rows)
    sp = jnp.concatenate([scaled(q_pairs[j, slot], prompt_pair(j * wide)) for j in range(pairs)])
    before = jnp.concatenate([top_all[k, mine, :] for k in heads])
    top = jnp.maximum(before, jnp.max(sp, axis=1, keepdims=True))
    ep = jnp.exp(sp - top[:, :1])
    keep = jnp.exp(before - top)
    more = jnp.sum(ep, axis=1, keepdims=True)
    for j in range(pairs):
        both = mix(ep[j * 2 * rows : (j + 1) * 2 * rows], prompt_pair(value_at + j * wide))
        for half in (0, 1):
            k = 2 * j + half
            part = slice(k * rows, (k + 1) * rows)
            added = both[half * rows : (half + 1) * rows, half * HEAD_SIZE : (half + 1) * HEAD_SIZE]
            sum_all[k, mine, :] = sum_all[k, mine, :] * keep[part] + more[part]
            acc[k, mine, :] = acc[k, mine, :] * keep[part] + added

    acc[...] = acc[...] / sum_all[...]
    for h in range(QUERY_HEADS):
        k, g = h // GROUP, h % GROUP
        out_ref[:, h * HEAD_SIZE : (h + 1) * HEAD_SIZE] = acc[
            k, pl.ds(g, new_rows, stride=GROUP), :
        ].astype(jnp.bfloat16)


def attend(joined, q_width, prompt, pool, table, lens, slot):
    blocks, tokens, width = joined.shape
    seqs = tokens // STEPS
    kv_width = width - q_width
    kv_off = q_width
    kv = joined
    if kv_width % (2 * HEAD_SIZE):
        kv = joined[:, :, q_width:].transpose(1, 0, 2).reshape(1, tokens, blocks * kv_width)
        prompt = prompt.transpose(1, 0, 2).reshape(1, prompt.shape[1], blocks * kv_width)
        kv_width, kv_off = blocks * kv_width, 0
    rows = seqs * STEPS * GROUP
    smem = pl.BlockSpec(memory_space=pltpu.SMEM)
    vmem = pl.BlockSpec(memory_space=pltpu.VMEM)
    kernel = functools.partial(
        attend_kernel, seqs=seqs, q_width=q_width, kv_off=kv_off, kv_width=kv_width, prompt_width=prompt.shape[2]
    )
    big = pltpu.VMEM((KEY_VALUE_HEADS, rows, HEAD_SIZE), jnp.float32)
    return pl.pallas_call(
        kernel,
        out_shape=jax.ShapeDtypeStruct((tokens, QUERY_HEADS * HEAD_SIZE), jnp.bfloat16),
        in_specs=[smem, smem, smem, vmem, vmem, vmem, pl.BlockSpec(memory_space=pl.ANY)],
        out_specs=vmem,
        scratch_shapes=[
            pltpu.VMEM((seqs, table.shape[1] * pool.shape[1], pool.shape[2]), jnp.bfloat16),
            pltpu.VMEM((KEY_VALUE_HEADS // 2, seqs, 2 * STEPS * GROUP, 2 * HEAD_SIZE), jnp.bfloat16),
            pltpu.VMEM((seqs, QUERY_HEADS * STEPS, tokens), jnp.float32),
            pltpu.VMEM((seqs, QUERY_HEADS * STEPS, tokens), jnp.bfloat16),
            big, big, big, big,
            pltpu.SemaphoreType.DMA((seqs, table.shape[1])),
        ],
        compiler_params=pltpu.CompilerParams(vmem_limit_bytes=ATTEND_LIMIT),
        name="attend",
    )(table.reshape(-1), lens, slot, joined, kv, prompt, pool)


def gather_blocks(own, axis, size):
    me = lax.axis_index(axis)
    line = size // 2
    place, side = me // 2, me % 2

    def hop(x, step, first, last):
        return lax.ppermute(
            x, axis, [(2 * c + p, 2 * (c + step) + p) for c in range(first, last + 1) for p in (0, 1)]
        )

    def swap(x, first, last):
        return lax.ppermute(x, axis, [(2 * c + p, 2 * c + 1 - p) for c in range(first, last + 1) for p in (0, 1)])

    up, down = {0: own}, {0: own}
    up_pair, down_pair = {}, {}
    near = swap(own, 0, line - 1)
    found = [((own,), 0, me), ((near,), 0, 2 * place + 1 - side)]
    for s in range(1, line):
        up[s] = hop(up[s - 1], 1, s - 1, line - 2)
        down[s] = hop(down[s - 1], -1, 1, line - s)
        up_pair[s] = swap(up[s], s, line - 1)
        down_pair[s] = swap(down[s], 0, line - 1 - s)
    for s in range(1, line):
        other = (place + line - s) % line
        first = place >= s
        found.append(((up[s], down[line - s]), 1 - first.astype(jnp.int32), 2 * other + side))
        found.append(((up_pair[s], down_pair[line - s]), 1 - first.astype(jnp.int32), 2 * other + 1 - side))
    return found, (up[line - 1], down[line - 1])


def project_kernel(owner_ref, choice_ref, *refs, tiles, counts):
    blocks = sum(counts)
    sources = refs[:blocks]
    wq_ref, wkv_ref, out_ref, x_here, w_here, x_sems, w_sems = refs[blocks:]
    size, tokens, _ = out_ref.shape
    q_width = wq_ref.shape[1]

    def fetch(j, source):
        rows = pl.ds(pl.multiple_of(owner_ref[j] * tokens, tokens), tokens)
        return pltpu.make_async_copy(source, x_here.at[rows], x_sems.at[j])

    at = 0
    firsts = []
    for j, count in enumerate(counts):
        firsts.append(sources[at])
        if count == 1:
            fetch(j, sources[at]).start()
        else:
            one, other = sources[at], sources[at + 1]

            @pl.when(choice_ref[j] == 0)
            def _():
                fetch(j, one).start()

            @pl.when(choice_ref[j] != 0)
            def _():
                fetch(j, other).start()

        at += count
    copies = []
    for i, (at, width) in enumerate(tiles):
        source = wq_ref.at[:, pl.ds(at, width)] if at < q_width else wkv_ref.at[:, pl.ds(at - q_width, width)]
        copies.append(pltpu.make_async_copy(source, w_here.at[:, pl.ds(at, width)], w_sems.at[i]))
    for c in copies[:AHEAD]:
        c.start()
    for j, source in enumerate(firsts):
        fetch(j, source).wait()

    for i, (at, width) in enumerate(tiles):
        copies[i].wait()
        if i + AHEAD < len(tiles):
            copies[i + AHEAD].start()
        cols = slice(at, at + width)
        y = jnp.dot(x_here[...], w_here[:, cols], preferred_element_type=jnp.float32).astype(jnp.bfloat16)
        for j in range(size):
            out_ref[j, :, cols] = y[j * tokens : (j + 1) * tokens]


def project(found, wq, wkv):
    size = len(found)
    tokens = found[0][0][0].shape[0]
    depth, q_width = wq.shape
    width = q_width + wkv.shape[1]
    wide = 2 * HEAD_SIZE
    tiles = [(at, min(wide, q_width - at)) for at in range(0, q_width, wide)]
    tiles += [(at, min(HEAD_SIZE, width - at)) for at in range(q_width, width, HEAD_SIZE)]
    counts = [len(options) for options, _, _ in found]
    sources = [block for options, _, _ in found for block in options]
    choices = jnp.stack([jnp.asarray(choice, jnp.int32) for _, choice, _ in found])
    owners = jnp.stack([jnp.asarray(owner, jnp.int32) for _, _, owner in found])
    smem = pl.BlockSpec(memory_space=pltpu.SMEM)
    vmem = pl.BlockSpec(memory_space=pltpu.VMEM)
    hbm = pl.BlockSpec(memory_space=pl.ANY)
    return pl.pallas_call(
        functools.partial(project_kernel, tiles=tiles, counts=counts),
        out_shape=jax.ShapeDtypeStruct((size, tokens, width), jnp.bfloat16),
        in_specs=[smem, smem] + [hbm] * len(sources) + [hbm, hbm],
        out_specs=vmem,
        scratch_shapes=[
            pltpu.VMEM((size * tokens, depth), wq.dtype),
            pltpu.VMEM((depth, width), wq.dtype),
            pltpu.SemaphoreType.DMA((size,)),
            pltpu.SemaphoreType.DMA((len(tiles),)),
        ],
        compiler_params=pltpu.CompilerParams(vmem_limit_bytes=PROJECT_LIMIT),
        cost_estimate=pl.CostEstimate(
            flops=2 * size * tokens * depth * width,
            bytes_accessed=2 * depth * (size * tokens + width),
            transcendentals=0,
        ),
        name="project",
    )(owners, choices, *sources, wq, wkv)


def per_device(size, hidden, wq, wkv, cache_pool, page_table, ctx_len, prompt_slot, prompt_kv):
    tokens = hidden.shape[0] * hidden.shape[1]
    own = hidden.reshape(tokens, hidden.shape[2])
    found, late = gather_blocks(own, "tensor", size)
    prompt_kv, _ = lax.optimization_barrier((prompt_kv, late))
    prompt = lax.all_to_all(prompt_kv, "tensor", split_axis=0, concat_axis=0, tiled=True)
    joined = project(found, wq, wkv)
    joined, prompt = lax.optimization_barrier((joined, prompt))
    back = lax.all_to_all(joined, "tensor", split_axis=0, concat_axis=0, tiled=True)
    out = attend(back, wq.shape[1], prompt, cache_pool, page_table, ctx_len, prompt_slot)
    return out.reshape(hidden.shape[0], hidden.shape[1], -1)


def solution(mesh):
    placed = (
        P(("groups", "tensor", "batch"), None, None),
        P(None, "tensor"),
        P(None, "tensor"),
        P(("groups", "tensor", "batch"), None, None),
        P(("groups", "tensor", "batch"), None),
        P(("groups", "tensor", "batch")),
        P(("groups", "tensor", "batch")),
        P(("groups", "batch"), None, "tensor"),
    )
    return jax.shard_map(
        functools.partial(per_device, mesh.shape["tensor"]),
        mesh=mesh,
        in_specs=placed,
        out_specs=P(("groups", "tensor", "batch"), None, None),
        check_vma=False,
    )
```

```python
import functools

import jax
import jax.numpy as jnp
from jax import lax
from jax.experimental import pallas as pl
from jax.experimental.pallas import tpu as pltpu
from jax.sharding import PartitionSpec as P


QUERY_HEADS = 64
KEY_VALUE_HEADS = 8
HEAD_SIZE = 128
GROUP = QUERY_HEADS // KEY_VALUE_HEADS
STEPS = 2
MASKED = -1e30
PROJECT_LIMIT = 48 << 20
AHEAD = 2
PAGES_AHEAD = 3
EARLY = 2
EARLY_LIMIT = 50 << 20
ATTEND_LIMIT = 50 << 20


def attend_kernel(
    table_ref, lens_ref, slot_ref, q_ref, kv_ref, prompt_ref, early_ref, pool_ref, out_ref,
    pages, q_pairs, new_scores, new_weights, acc, top_all, sum_all, q_f32, sems,
    *, seqs, q_width, kv_off, kv_width, prompt_width,
):
    span_pages = table_ref.shape[0] // seqs
    page_rows = pool_ref.shape[1]
    span = span_pages * page_rows
    early = early_ref.shape[0]
    rows = STEPS * GROUP
    new_rows = seqs * STEPS
    all_rows = KEY_VALUE_HEADS * rows
    pairs = KEY_VALUE_HEADS // 2
    wide = 2 * HEAD_SIZE
    value_at = KEY_VALUE_HEADS * HEAD_SIZE
    heads = range(KEY_VALUE_HEADS)

    def page_copy(s, p):
        return pltpu.make_async_copy(
            pool_ref.at[table_ref[s * span_pages + p]],
            pages.at[s - early, pl.ds(p * page_rows, page_rows)],
            sems.at[s - early, p],
        )

    for s in range(early, min(early + PAGES_AHEAD, seqs)):
        for p in range(span_pages):
            page_copy(s, p).start()

    def new_pair(col):
        block, at = col // kv_width, kv_off + col % kv_width
        return kv_ref[block, :, at : at + wide]

    def prompt_pair(col):
        block, at = col // prompt_width, col % prompt_width
        return prompt_ref[block, :, at : at + wide]

    def scaled(q, keys):
        return lax.dot_general(
            q, keys, (((1,), (1,)), ((), ())), preferred_element_type=jnp.float32
        ) * HEAD_SIZE ** (-0.5)

    def mix(w, values):
        return jnp.dot(w.astype(jnp.bfloat16), values, preferred_element_type=jnp.float32)

    for h in range(QUERY_HEADS):
        k, g = h // GROUP, h % GROUP
        block, at = (h * HEAD_SIZE) // q_width, (h * HEAD_SIZE) % q_width
        q_f32[k, pl.ds(g, new_rows, stride=GROUP), :] = q_ref[block, :, at : at + HEAD_SIZE].astype(jnp.float32)
    blank = jnp.zeros((seqs, rows, HEAD_SIZE), jnp.bfloat16)
    for k in heads:
        j, half = k // 2, k % 2
        mine = slice(half * rows, (half + 1) * rows)
        q_pairs[j, :, mine, half * HEAD_SIZE : (half + 1) * HEAD_SIZE] = (
            q_f32[k].astype(jnp.bfloat16).reshape(seqs, rows, HEAD_SIZE)
        )
        q_pairs[j, :, mine, (1 - half) * HEAD_SIZE : (2 - half) * HEAD_SIZE] = blank

    step_of = (lax.broadcasted_iota(jnp.int32, (seqs, 2 * rows, new_rows), 1) // GROUP) % STEPS
    seq_of = lax.broadcasted_iota(jnp.int32, (seqs, 2 * rows, new_rows), 0)
    offset = lax.broadcasted_iota(jnp.int32, (seqs, 2 * rows, new_rows), 2) - seq_of * STEPS
    live_new = (offset >= 0) & (offset <= step_of)
    for j in range(pairs):
        sn = scaled(q_pairs[j].reshape(seqs * 2 * rows, wide), new_pair(j * wide))
        new_scores[:, j * 2 * rows : (j + 1) * 2 * rows, :] = jnp.where(
            live_new, sn.reshape(seqs, 2 * rows, new_rows), MASKED
        )

    where_key = lax.broadcasted_iota(jnp.int32, (all_rows, span), 1)

    def one_sequence(s, context):
        at = pl.multiple_of(s * rows, rows)
        sc = jnp.concatenate(
            [scaled(q_pairs[j, s], context[:, j * wide : (j + 1) * wide]) for j in range(pairs)]
        )
        sc = jnp.where(where_key < lens_ref[s], sc, MASKED)
        sn = new_scores[s]
        top = jnp.maximum(jnp.max(sc, axis=1, keepdims=True), jnp.max(sn, axis=1, keepdims=True))
        ec = jnp.exp(sc - top)
        en = jnp.exp(sn - top)
        total = jnp.sum(ec, axis=1, keepdims=True) + jnp.sum(en, axis=1, keepdims=True)
        new_weights[s] = en.astype(jnp.bfloat16)
        for j in range(pairs):
            col = value_at + j * wide
            both = mix(ec[j * 2 * rows : (j + 1) * 2 * rows], context[:, col : col + wide])
            acc[2 * j, pl.ds(at, rows), :] = both[:rows, :HEAD_SIZE]
            acc[2 * j + 1, pl.ds(at, rows), :] = both[rows:, HEAD_SIZE:]
        for k in heads:
            part = slice(k * rows, (k + 1) * rows)
            top_all[k, pl.ds(at, rows), :] = jnp.broadcast_to(top[part], (rows, HEAD_SIZE))
            sum_all[k, pl.ds(at, rows), :] = jnp.broadcast_to(total[part], (rows, HEAD_SIZE))

    @pl.loop(0, early)
    def _(s):
        one_sequence(s, early_ref.at[s])

    @pl.loop(early, seqs)
    def _(s):
        @pl.when(s + PAGES_AHEAD < seqs)
        def _():
            for p in range(span_pages):
                page_copy(s + PAGES_AHEAD, p).start()

        for p in range(span_pages):
            page_copy(s, p).wait()
        one_sequence(s, pages.at[s - early])

    for j in range(pairs):
        w = new_weights[:, j * 2 * rows : (j + 1) * 2 * rows, :].reshape(seqs * 2 * rows, new_rows)
        both = mix(w, new_pair(value_at + j * wide)).reshape(seqs, 2 * rows, wide)
        acc[2 * j] += both[:, :rows, :HEAD_SIZE].reshape(seqs * rows, HEAD_SIZE)
        acc[2 * j + 1] += both[:, rows:, HEAD_SIZE:].reshape(seqs * rows, HEAD_SIZE)

    slot = slot_ref[0]
    mine = pl.ds(pl.multiple_of(slot * rows, rows), rows)
    sp = jnp.concatenate([scaled(q_pairs[j, slot], prompt_pair(j * wide)) for j in range(pairs)])
    before = jnp.concatenate([top_all[k, mine, :] for k in heads])
    top = jnp.maximum(before, jnp.max(sp, axis=1, keepdims=True))
    ep = jnp.exp(sp - top[:, :1])
    keep = jnp.exp(before - top)
    more = jnp.sum(ep, axis=1, keepdims=True)
    for j in range(pairs):
        both = mix(ep[j * 2 * rows : (j + 1) * 2 * rows], prompt_pair(value_at + j * wide))
        for half in (0, 1):
            k = 2 * j + half
            part = slice(k * rows, (k + 1) * rows)
            added = both[half * rows : (half + 1) * rows, half * HEAD_SIZE : (half + 1) * HEAD_SIZE]
            sum_all[k, mine, :] = sum_all[k, mine, :] * keep[part] + more[part]
            acc[k, mine, :] = acc[k, mine, :] * keep[part] + added

    acc[...] = acc[...] / sum_all[...]
    for h in range(QUERY_HEADS):
        k, g = h // GROUP, h % GROUP
        head = acc[k, pl.ds(g, new_rows, stride=GROUP), :].astype(jnp.bfloat16)
        out_ref[:, :, h * HEAD_SIZE : (h + 1) * HEAD_SIZE] = head.reshape(seqs, STEPS, HEAD_SIZE)


def attend(joined, q_width, prompt, early, pool, table, lens, slot):
    blocks, tokens, width = joined.shape
    seqs = tokens // STEPS
    kv_width = width - q_width
    kv_off = q_width
    kv = joined
    if kv_width % (2 * HEAD_SIZE):
        kv = joined[:, :, q_width:].transpose(1, 0, 2).reshape(1, tokens, blocks * kv_width)
        prompt = prompt.transpose(1, 0, 2).reshape(1, prompt.shape[1], blocks * kv_width)
        kv_width, kv_off = blocks * kv_width, 0
    rows = seqs * STEPS * GROUP
    smem = pl.BlockSpec(memory_space=pltpu.SMEM)
    vmem = pl.BlockSpec(memory_space=pltpu.VMEM)
    kernel = functools.partial(
        attend_kernel, seqs=seqs, q_width=q_width, kv_off=kv_off, kv_width=kv_width, prompt_width=prompt.shape[2]
    )
    big = pltpu.VMEM((KEY_VALUE_HEADS, rows, HEAD_SIZE), jnp.float32)
    return pl.pallas_call(
        kernel,
        out_shape=jax.ShapeDtypeStruct((seqs, STEPS, QUERY_HEADS * HEAD_SIZE), jnp.bfloat16),
        in_specs=[smem, smem, smem, vmem, vmem, vmem, vmem, pl.BlockSpec(memory_space=pl.ANY)],
        out_specs=vmem,
        scratch_shapes=[
            pltpu.VMEM((seqs - early.shape[0], table.shape[1] * pool.shape[1], pool.shape[2]), jnp.bfloat16),
            pltpu.VMEM((KEY_VALUE_HEADS // 2, seqs, 2 * STEPS * GROUP, 2 * HEAD_SIZE), jnp.bfloat16),
            pltpu.VMEM((seqs, QUERY_HEADS * STEPS, tokens), jnp.float32),
            pltpu.VMEM((seqs, QUERY_HEADS * STEPS, tokens), jnp.bfloat16),
            big, big, big, big,
            pltpu.SemaphoreType.DMA((seqs - early.shape[0], table.shape[1])),
        ],
        compiler_params=pltpu.CompilerParams(vmem_limit_bytes=ATTEND_LIMIT),
        name="attend",
    )(table.reshape(-1), lens, slot, joined, kv, prompt, early, pool)


def early_kernel(table_ref, token_ref, pool_ref, out_ref, sems):
    page_rows = pool_ref.shape[1]
    each = out_ref.shape[1] // page_rows
    copies = [
        pltpu.make_async_copy(
            pool_ref.at[table_ref[s * each + p]], out_ref.at[s, pl.ds(p * page_rows, page_rows)], sems.at[s, p]
        )
        for s in range(out_ref.shape[0])
        for p in range(each)
    ]
    for c in copies:
        c.start()
    for c in copies:
        c.wait()


def early_pages(token, table, pool):
    seqs, each = min(EARLY, table.shape[0]), table.shape[1]
    hbm = pl.BlockSpec(memory_space=pl.ANY)
    shape = (seqs, each * pool.shape[1], pool.shape[2])
    return pl.pallas_call(
        early_kernel,
        out_shape=pltpu.VMEM(shape, pool.dtype),
        in_specs=[pl.BlockSpec(memory_space=pltpu.SMEM), hbm, hbm],
        out_specs=pl.BlockSpec(memory_space=pltpu.VMEM),
        scratch_shapes=[pltpu.SemaphoreType.DMA((seqs, each))],
        compiler_params=pltpu.CompilerParams(vmem_limit_bytes=EARLY_LIMIT),
        cost_estimate=pl.CostEstimate(flops=0, bytes_accessed=4 * shape[0] * shape[1] * shape[2], transcendentals=0),
        name="early",
    )(table.reshape(-1), token, pool)


def gather_blocks(own, axis, size):
    me = lax.axis_index(axis)
    line = size // 2
    place, side = me // 2, me % 2

    def hop(x, step, first, last):
        return lax.ppermute(
            x, axis, [(2 * c + p, 2 * (c + step) + p) for c in range(first, last + 1) for p in (0, 1)]
        )

    def swap(x, first, last):
        return lax.ppermute(x, axis, [(2 * c + p, 2 * c + 1 - p) for c in range(first, last + 1) for p in (0, 1)])

    up, down = {0: own}, {0: own}
    up_pair, down_pair = {}, {}
    near = swap(own, 0, line - 1)
    found = [((own,), 0, me), ((near,), 0, 2 * place + 1 - side)]
    for s in range(1, line - 1):
        up[s] = hop(up[s - 1], 1, s - 1, line - 2)
        down[s] = hop(down[s - 1], -1, 1, line - s)
        if s < line - 2:
            up_pair[s] = swap(up[s], s, line - 1)
            down_pair[s] = swap(down[s], 0, line - 1 - s)
    both = jnp.where(2 * place >= line, up[line - 2], down[line - 2])
    ends = [(1, 0), (line - 2, line - 1)]
    up[line - 1] = down[line - 1] = lax.ppermute(both, axis, [(2 * a + p, 2 * b + p) for a, b in ends for p in (0, 1)])
    up_pair[line - 2] = down_pair[line - 2] = lax.ppermute(
        both, axis, [(2 * c + p, 2 * c + 1 - p) for c in (0, 1, line - 2, line - 1) for p in (0, 1)]
    )
    up_pair[line - 1] = down_pair[line - 1] = lax.ppermute(
        up[line - 1], axis, [(2 * c + p, 2 * c + 1 - p) for c in (0, line - 1) for p in (0, 1)]
    )
    for s in range(1, line):
        other = (place + line - s) % line
        first = place >= s
        found.append(((up[s], down[line - s]), 1 - first.astype(jnp.int32), 2 * other + side))
        found.append(((up_pair[s], down_pair[line - s]), 1 - first.astype(jnp.int32), 2 * other + 1 - side))
    return found, (up[line - 1], down[line - 1])


def project_kernel(owner_ref, choice_ref, *refs, tiles, counts):
    blocks = sum(counts)
    sources = refs[:blocks]
    wq_ref, wkv_ref, out_ref, x_here, w_here, x_sems, w_sems = refs[blocks:]
    size, tokens, _ = out_ref.shape
    q_width = wq_ref.shape[1]

    def fetch(j, source):
        rows = pl.ds(pl.multiple_of(owner_ref[j] * tokens, tokens), tokens)
        return pltpu.make_async_copy(source, x_here.at[rows], x_sems.at[j])

    at = 0
    firsts = []
    for j, count in enumerate(counts):
        firsts.append(sources[at])
        if count == 1:
            fetch(j, sources[at]).start()
        else:
            one, other = sources[at], sources[at + 1]

            @pl.when(choice_ref[j] == 0)
            def _():
                fetch(j, one).start()

            @pl.when(choice_ref[j] != 0)
            def _():
                fetch(j, other).start()

        at += count
    copies = []
    for i, (at, width) in enumerate(tiles):
        source = wq_ref.at[:, pl.ds(at, width)] if at < q_width else wkv_ref.at[:, pl.ds(at - q_width, width)]
        copies.append(pltpu.make_async_copy(source, w_here.at[:, pl.ds(at, width)], w_sems.at[i]))
    for c in copies[:AHEAD]:
        c.start()
    for j, source in enumerate(firsts):
        fetch(j, source).wait()

    for i, (at, width) in enumerate(tiles):
        copies[i].wait()
        if i + AHEAD < len(tiles):
            copies[i + AHEAD].start()
        cols = slice(at, at + width)
        y = jnp.dot(x_here[...], w_here[:, cols], preferred_element_type=jnp.float32).astype(jnp.bfloat16)
        for j in range(size):
            out_ref[j, :, cols] = y[j * tokens : (j + 1) * tokens]


def project(found, wq, wkv):
    size = len(found)
    tokens = found[0][0][0].shape[0]
    depth, q_width = wq.shape
    width = q_width + wkv.shape[1]
    wide = 2 * HEAD_SIZE
    tiles = [(at, min(wide, q_width - at)) for at in range(0, q_width, wide)]
    tiles += [(at, min(HEAD_SIZE, width - at)) for at in range(q_width, width, HEAD_SIZE)]
    counts = [len(options) for options, _, _ in found]
    sources = [block for options, _, _ in found for block in options]
    choices = jnp.stack([jnp.asarray(choice, jnp.int32) for _, choice, _ in found])
    owners = jnp.stack([jnp.asarray(owner, jnp.int32) for _, _, owner in found])
    smem = pl.BlockSpec(memory_space=pltpu.SMEM)
    vmem = pl.BlockSpec(memory_space=pltpu.VMEM)
    hbm = pl.BlockSpec(memory_space=pl.ANY)
    return pl.pallas_call(
        functools.partial(project_kernel, tiles=tiles, counts=counts),
        out_shape=jax.ShapeDtypeStruct((size, tokens, width), jnp.bfloat16),
        in_specs=[smem, smem] + [hbm] * len(sources) + [hbm, hbm],
        out_specs=vmem,
        scratch_shapes=[
            pltpu.VMEM((size * tokens, depth), wq.dtype),
            pltpu.VMEM((depth, width), wq.dtype),
            pltpu.SemaphoreType.DMA((size,)),
            pltpu.SemaphoreType.DMA((len(tiles),)),
        ],
        compiler_params=pltpu.CompilerParams(vmem_limit_bytes=PROJECT_LIMIT),
        cost_estimate=pl.CostEstimate(
            flops=2 * size * tokens * depth * width,
            bytes_accessed=2 * depth * (size * tokens + width),
            transcendentals=0,
        ),
        name="project",
    )(owners, choices, *sources, wq, wkv)


def per_device(size, hidden, wq, wkv, cache_pool, page_table, ctx_len, prompt_slot, prompt_kv):
    tokens = hidden.shape[0] * hidden.shape[1]
    own = hidden.reshape(tokens, hidden.shape[2])
    found, late = gather_blocks(own, "tensor", size)
    prompt_kv, _ = lax.optimization_barrier((prompt_kv, late))
    prompt = lax.all_to_all(prompt_kv, "tensor", split_axis=0, concat_axis=0, tiled=True)
    joined = project(found, wq, wkv)
    joined, prompt = lax.optimization_barrier((joined, prompt))
    back = lax.all_to_all(joined, "tensor", split_axis=0, concat_axis=0, tiled=True)
    early = early_pages(joined, page_table, cache_pool)
    return attend(back, wq.shape[1], prompt, early, cache_pool, page_table, ctx_len, prompt_slot)


def solution(mesh):
    placed = (
        P(("groups", "tensor", "batch"), None, None),
        P(None, "tensor"),
        P(None, "tensor"),
        P(("groups", "tensor", "batch"), None, None),
        P(("groups", "tensor", "batch"), None),
        P(("groups", "tensor", "batch")),
        P(("groups", "tensor", "batch")),
        P(("groups", "batch"), None, "tensor"),
    )
    return jax.shard_map(
        functools.partial(per_device, mesh.shape["tensor"]),
        mesh=mesh,
        in_specs=placed,
        out_specs=P(("groups", "tensor", "batch"), None, None),
        check_vma=False,
    )
```

```python
import functools

import jax
import jax.numpy as jnp
from jax import lax
from jax.experimental import pallas as pl
from jax.experimental.pallas import tpu as pltpu
from jax.sharding import PartitionSpec as P


QUERY_HEADS = 64
KEY_VALUE_HEADS = 8
HEAD_SIZE = 128
GROUP = QUERY_HEADS // KEY_VALUE_HEADS
STEPS = 2
MASKED = -1e30
PROJECT_LIMIT = 48 << 20
AHEAD = 2
LANES = 512
PAGES_AHEAD = 3
EARLY = 2
EARLY_LIMIT = 50 << 20
ATTEND_LIMIT = 50 << 20


def attend_kernel(
    table_ref, lens_ref, slot_ref, q_ref, kv_ref, prompt_ref, early_ref, pool_ref, out_ref,
    pages, q_pairs, new_scores, new_weights, acc, top_all, sum_all, q_f32, sems,
    *, seqs, q_width, kv_off, kv_width, prompt_width,
):
    span_pages = table_ref.shape[0] // seqs
    page_rows = pool_ref.shape[1]
    span = span_pages * page_rows
    early = early_ref.shape[0]
    rows = STEPS * GROUP
    new_rows = seqs * STEPS
    all_rows = KEY_VALUE_HEADS * rows
    pairs = KEY_VALUE_HEADS // 2
    wide = 2 * HEAD_SIZE
    value_at = KEY_VALUE_HEADS * HEAD_SIZE
    heads = range(KEY_VALUE_HEADS)

    def page_copy(s, p):
        return pltpu.make_async_copy(
            pool_ref.at[table_ref[s * span_pages + p]],
            pages.at[s - early, pl.ds(p * page_rows, page_rows)],
            sems.at[s - early, p],
        )

    for s in range(early, min(early + PAGES_AHEAD, seqs)):
        for p in range(span_pages):
            page_copy(s, p).start()

    def new_pair(col):
        block, at = col // kv_width, kv_off + col % kv_width
        return kv_ref[block, :, at : at + wide]

    def prompt_pair(col):
        block, at = col // prompt_width, col % prompt_width
        return prompt_ref[block, :, at : at + wide]

    def scaled(q, keys):
        return lax.dot_general(
            q, keys, (((1,), (1,)), ((), ())), preferred_element_type=jnp.float32
        ) * HEAD_SIZE ** (-0.5)

    def mix(w, values):
        return jnp.dot(w.astype(jnp.bfloat16), values, preferred_element_type=jnp.float32)

    for h in range(QUERY_HEADS):
        k, g = h // GROUP, h % GROUP
        block, at = (h * HEAD_SIZE) // q_width, (h * HEAD_SIZE) % q_width
        q_f32[k, pl.ds(g, new_rows, stride=GROUP), :] = q_ref[block, :, at : at + HEAD_SIZE].astype(jnp.float32)
    blank = jnp.zeros((seqs, rows, HEAD_SIZE), jnp.bfloat16)
    for k in heads:
        j, half = k // 2, k % 2
        mine = slice(half * rows, (half + 1) * rows)
        q_pairs[j, :, mine, half * HEAD_SIZE : (half + 1) * HEAD_SIZE] = (
            q_f32[k].astype(jnp.bfloat16).reshape(seqs, rows, HEAD_SIZE)
        )
        q_pairs[j, :, mine, (1 - half) * HEAD_SIZE : (2 - half) * HEAD_SIZE] = blank

    step_of = (lax.broadcasted_iota(jnp.int32, (seqs, 2 * rows, new_rows), 1) // GROUP) % STEPS
    seq_of = lax.broadcasted_iota(jnp.int32, (seqs, 2 * rows, new_rows), 0)
    offset = lax.broadcasted_iota(jnp.int32, (seqs, 2 * rows, new_rows), 2) - seq_of * STEPS
    live_new = (offset >= 0) & (offset <= step_of)
    for j in range(pairs):
        sn = scaled(q_pairs[j].reshape(seqs * 2 * rows, wide), new_pair(j * wide))
        new_scores[:, j * 2 * rows : (j + 1) * 2 * rows, :] = jnp.where(
            live_new, sn.reshape(seqs, 2 * rows, new_rows), MASKED
        )

    where_key = lax.broadcasted_iota(jnp.int32, (all_rows, span), 1)

    def context_of(s):
        if s < early:
            return early_ref.at[s]
        return pages.at[s - early]

    def cached_scores(s):
        if s >= early:
            if s + PAGES_AHEAD < seqs:
                for p in range(span_pages):
                    page_copy(s + PAGES_AHEAD, p).start()
            for p in range(span_pages):
                page_copy(s, p).wait()
        context = context_of(s)
        sc = jnp.concatenate(
            [scaled(q_pairs[j, s], context[:, j * wide : (j + 1) * wide]) for j in range(pairs)]
        )
        return jnp.where(where_key < lens_ref[s], sc, MASKED)

    def one_sequence(s, sc):
        part_rows = slice(s * rows, (s + 1) * rows)
        context = context_of(s)
        sn = new_scores[s]
        top = jnp.maximum(jnp.max(sc, axis=1, keepdims=True), jnp.max(sn, axis=1, keepdims=True))
        ec = jnp.exp(sc - top)
        en = jnp.exp(sn - top)
        total = jnp.sum(ec, axis=1, keepdims=True) + jnp.sum(en, axis=1, keepdims=True)
        new_weights[s] = en.astype(jnp.bfloat16)
        for j in range(pairs):
            col = value_at + j * wide
            both = mix(ec[j * 2 * rows : (j + 1) * 2 * rows], context[:, col : col + wide])
            acc[2 * j, part_rows, :] = both[:rows, :HEAD_SIZE]
            acc[2 * j + 1, part_rows, :] = both[rows:, HEAD_SIZE:]
        for k in heads:
            part = slice(k * rows, (k + 1) * rows)
            top_all[k, part_rows, :] = jnp.broadcast_to(top[part], (rows, HEAD_SIZE))
            sum_all[k, part_rows, :] = jnp.broadcast_to(total[part], (rows, HEAD_SIZE))

    scores = cached_scores(0)
    for s in range(seqs):
        following = cached_scores(s + 1) if s + 1 < seqs else None
        one_sequence(s, scores)
        scores = following

    for j in range(pairs):
        w = new_weights[:, j * 2 * rows : (j + 1) * 2 * rows, :].reshape(seqs * 2 * rows, new_rows)
        both = mix(w, new_pair(value_at + j * wide)).reshape(seqs, 2 * rows, wide)
        acc[2 * j] += both[:, :rows, :HEAD_SIZE].reshape(seqs * rows, HEAD_SIZE)
        acc[2 * j + 1] += both[:, rows:, HEAD_SIZE:].reshape(seqs * rows, HEAD_SIZE)

    slot = slot_ref[0]
    mine = pl.ds(pl.multiple_of(slot * rows, rows), rows)
    sp = jnp.concatenate([scaled(q_pairs[j, slot], prompt_pair(j * wide)) for j in range(pairs)])
    before = jnp.concatenate([top_all[k, mine, :] for k in heads])
    top = jnp.maximum(before, jnp.max(sp, axis=1, keepdims=True))
    ep = jnp.exp(sp - top[:, :1])
    keep = jnp.exp(before - top)
    more = jnp.sum(ep, axis=1, keepdims=True)
    for j in range(pairs):
        both = mix(ep[j * 2 * rows : (j + 1) * 2 * rows], prompt_pair(value_at + j * wide))
        for half in (0, 1):
            k = 2 * j + half
            part = slice(k * rows, (k + 1) * rows)
            added = both[half * rows : (half + 1) * rows, half * HEAD_SIZE : (half + 1) * HEAD_SIZE]
            sum_all[k, mine, :] = sum_all[k, mine, :] * keep[part] + more[part]
            acc[k, mine, :] = acc[k, mine, :] * keep[part] + added

    acc[...] = acc[...] / sum_all[...]
    for h in range(QUERY_HEADS):
        k, g = h // GROUP, h % GROUP
        head = acc[k, pl.ds(g, new_rows, stride=GROUP), :].astype(jnp.bfloat16)
        out_ref[:, :, h * HEAD_SIZE : (h + 1) * HEAD_SIZE] = head.reshape(seqs, STEPS, HEAD_SIZE)


def attend(joined, q_width, prompt, early, pool, table, lens, slot):
    blocks, tokens, width = joined.shape
    seqs = tokens // STEPS
    kv_width = width - q_width
    kv_off = q_width
    kv = joined
    if kv_width % (2 * HEAD_SIZE):
        kv = joined[:, :, q_width:].transpose(1, 0, 2).reshape(1, tokens, blocks * kv_width)
        prompt = prompt.transpose(1, 0, 2).reshape(1, prompt.shape[1], blocks * kv_width)
        kv_width, kv_off = blocks * kv_width, 0
    rows = seqs * STEPS * GROUP
    smem = pl.BlockSpec(memory_space=pltpu.SMEM)
    vmem = pl.BlockSpec(memory_space=pltpu.VMEM)
    kernel = functools.partial(
        attend_kernel, seqs=seqs, q_width=q_width, kv_off=kv_off, kv_width=kv_width, prompt_width=prompt.shape[2]
    )
    big = pltpu.VMEM((KEY_VALUE_HEADS, rows, HEAD_SIZE), jnp.float32)
    return pl.pallas_call(
        kernel,
        out_shape=jax.ShapeDtypeStruct((seqs, STEPS, QUERY_HEADS * HEAD_SIZE), jnp.bfloat16),
        in_specs=[smem, smem, smem, vmem, vmem, vmem, vmem, pl.BlockSpec(memory_space=pl.ANY)],
        out_specs=vmem,
        scratch_shapes=[
            pltpu.VMEM((seqs - early.shape[0], table.shape[1] * pool.shape[1], pool.shape[2]), jnp.bfloat16),
            pltpu.VMEM((KEY_VALUE_HEADS // 2, seqs, 2 * STEPS * GROUP, 2 * HEAD_SIZE), jnp.bfloat16),
            pltpu.VMEM((seqs, QUERY_HEADS * STEPS, tokens), jnp.float32),
            pltpu.VMEM((seqs, QUERY_HEADS * STEPS, tokens), jnp.bfloat16),
            big, big, big, big,
            pltpu.SemaphoreType.DMA((seqs - early.shape[0], table.shape[1])),
        ],
        compiler_params=pltpu.CompilerParams(vmem_limit_bytes=ATTEND_LIMIT),
        name="attend",
    )(table.reshape(-1), lens, slot, joined, kv, prompt, early, pool)


def early_kernel(table_ref, token_ref, pool_ref, out_ref, sems):
    page_rows = pool_ref.shape[1]
    each = out_ref.shape[1] // page_rows
    copies = [
        pltpu.make_async_copy(
            pool_ref.at[table_ref[s * each + p]], out_ref.at[s, pl.ds(p * page_rows, page_rows)], sems.at[s, p]
        )
        for s in range(out_ref.shape[0])
        for p in range(each)
    ]
    for c in copies:
        c.start()
    for c in copies:
        c.wait()


def early_pages(token, table, pool):
    seqs, each = min(EARLY, table.shape[0]), table.shape[1]
    hbm = pl.BlockSpec(memory_space=pl.ANY)
    shape = (seqs, each * pool.shape[1], pool.shape[2])
    return pl.pallas_call(
        early_kernel,
        out_shape=pltpu.VMEM(shape, pool.dtype),
        in_specs=[pl.BlockSpec(memory_space=pltpu.SMEM), hbm, hbm],
        out_specs=pl.BlockSpec(memory_space=pltpu.VMEM),
        scratch_shapes=[pltpu.SemaphoreType.DMA((seqs, each))],
        compiler_params=pltpu.CompilerParams(vmem_limit_bytes=EARLY_LIMIT),
        cost_estimate=pl.CostEstimate(flops=0, bytes_accessed=4 * shape[0] * shape[1] * shape[2], transcendentals=0),
        name="early",
    )(table.reshape(-1), token, pool)


def gather_blocks(own, axis, size):
    me = lax.axis_index(axis)
    line = size // 2
    place, side = me // 2, me % 2

    def hop(x, step, first, last):
        return lax.ppermute(
            x, axis, [(2 * c + p, 2 * (c + step) + p) for c in range(first, last + 1) for p in (0, 1)]
        )

    def swap(x, first, last):
        return lax.ppermute(x, axis, [(2 * c + p, 2 * c + 1 - p) for c in range(first, last + 1) for p in (0, 1)])

    up, down = {0: own}, {0: own}
    up_pair, down_pair = {}, {}
    near = swap(own, 0, line - 1)
    found = [((own,), 0, me), ((near,), 0, 2 * place + 1 - side)]
    for s in range(1, line - 1):
        up[s] = hop(up[s - 1], 1, s - 1, line - 2)
        down[s] = hop(down[s - 1], -1, 1, line - s)
        if s < line - 2:
            up_pair[s] = swap(up[s], s, line - 1)
            down_pair[s] = swap(down[s], 0, line - 1 - s)
    both = jnp.where(2 * place >= line, up[line - 2], down[line - 2])
    ends = [(1, 0), (line - 2, line - 1)]
    up[line - 1] = down[line - 1] = lax.ppermute(both, axis, [(2 * a + p, 2 * b + p) for a, b in ends for p in (0, 1)])
    up_pair[line - 2] = down_pair[line - 2] = lax.ppermute(
        both, axis, [(2 * c + p, 2 * c + 1 - p) for c in (0, 1, line - 2, line - 1) for p in (0, 1)]
    )
    up_pair[line - 1] = down_pair[line - 1] = lax.ppermute(
        up[line - 1], axis, [(2 * c + p, 2 * c + 1 - p) for c in (0, line - 1) for p in (0, 1)]
    )
    for s in range(1, line):
        other = (place + line - s) % line
        first = place >= s
        found.append(((up[s], down[line - s]), 1 - first.astype(jnp.int32), 2 * other + side))
        found.append(((up_pair[s], down_pair[line - s]), 1 - first.astype(jnp.int32), 2 * other + 1 - side))
    return found, (up[line - 1], down[line - 1])


def project_kernel(owner_ref, choice_ref, *refs, tiles, counts):
    blocks = sum(counts)
    sources = refs[:blocks]
    wq_ref, wkv_ref, out_ref, x_raw, x_here, w_here, x_sems, w_sems = refs[blocks:]
    size, tokens, _ = out_ref.shape
    seqs = sources[0].shape[0]
    q_width = wq_ref.shape[1]

    def fetch(j, source):
        return pltpu.make_async_copy(source, x_raw.at[pl.ds(owner_ref[j] * seqs, seqs)], x_sems.at[j])

    at = 0
    firsts = []
    for j, count in enumerate(counts):
        firsts.append(sources[at])
        if count == 1:
            fetch(j, sources[at]).start()
        else:
            one, other = sources[at], sources[at + 1]

            @pl.when(choice_ref[j] == 0)
            def _():
                fetch(j, one).start()

            @pl.when(choice_ref[j] != 0)
            def _():
                fetch(j, other).start()

        at += count
    copies = []
    for i, (at, width) in enumerate(tiles):
        source = wq_ref.at[:, pl.ds(at, width)] if at < q_width else wkv_ref.at[:, pl.ds(at - q_width, width)]
        copies.append(pltpu.make_async_copy(source, w_here.at[:, pl.ds(at, width)], w_sems.at[i]))
    for c in copies[:AHEAD]:
        c.start()
    for j, source in enumerate(firsts):
        fetch(j, source).wait()

    @pl.loop(0, x_raw.shape[2] // LANES)
    def _(c):
        cols = pl.ds(pl.multiple_of(c * LANES, LANES), LANES)
        x_here[:, cols] = x_raw[:, :, cols].reshape(size * tokens, LANES)

    for i, (at, width) in enumerate(tiles):
        copies[i].wait()
        if i + AHEAD < len(tiles):
            copies[i + AHEAD].start()
        cols = slice(at, at + width)
        y = jnp.dot(x_here[...], w_here[:, cols], preferred_element_type=jnp.float32).astype(jnp.bfloat16)
        for j in range(size):
            out_ref[j, :, cols] = y[j * tokens : (j + 1) * tokens]


def project(found, wq, wkv):
    size = len(found)
    block = found[0][0][0].shape
    tokens = block[0] * block[1]
    depth, q_width = wq.shape
    width = q_width + wkv.shape[1]
    wide = 2 * HEAD_SIZE
    tiles = [(at, min(wide, q_width - at)) for at in range(0, q_width, wide)]
    tiles += [(at, min(HEAD_SIZE, width - at)) for at in range(q_width, width, HEAD_SIZE)]
    counts = [len(options) for options, _, _ in found]
    sources = [block for options, _, _ in found for block in options]
    choices = jnp.stack([jnp.asarray(choice, jnp.int32) for _, choice, _ in found])
    owners = jnp.stack([jnp.asarray(owner, jnp.int32) for _, _, owner in found])
    smem = pl.BlockSpec(memory_space=pltpu.SMEM)
    vmem = pl.BlockSpec(memory_space=pltpu.VMEM)
    hbm = pl.BlockSpec(memory_space=pl.ANY)
    return pl.pallas_call(
        functools.partial(project_kernel, tiles=tiles, counts=counts),
        out_shape=jax.ShapeDtypeStruct((size, tokens, width), jnp.bfloat16),
        in_specs=[smem, smem] + [hbm] * len(sources) + [hbm, hbm],
        out_specs=vmem,
        scratch_shapes=[
            pltpu.VMEM((size * block[0], block[1], depth), wq.dtype),
            pltpu.VMEM((size * tokens, depth), wq.dtype),
            pltpu.VMEM((depth, width), wq.dtype),
            pltpu.SemaphoreType.DMA((size,)),
            pltpu.SemaphoreType.DMA((len(tiles),)),
        ],
        compiler_params=pltpu.CompilerParams(vmem_limit_bytes=PROJECT_LIMIT),
        cost_estimate=pl.CostEstimate(
            flops=2 * size * tokens * depth * width,
            bytes_accessed=2 * depth * (size * tokens + width),
            transcendentals=0,
        ),
        name="project",
    )(owners, choices, pltpu.with_memory_space_constraint(sources[0], pltpu.HBM), *sources[1:], wq, wkv)


def per_device(size, hidden, wq, wkv, cache_pool, page_table, ctx_len, prompt_slot, prompt_kv):
    found, late = gather_blocks(hidden, "tensor", size)
    prompt_kv, _ = lax.optimization_barrier((prompt_kv, late))
    prompt = lax.all_to_all(prompt_kv, "tensor", split_axis=0, concat_axis=0, tiled=True)
    joined = project(found, wq, wkv)
    joined, prompt = lax.optimization_barrier((joined, prompt))
    back = lax.all_to_all(joined, "tensor", split_axis=0, concat_axis=0, tiled=True)
    early = early_pages(joined, page_table, cache_pool)
    return attend(back, wq.shape[1], prompt, early, cache_pool, page_table, ctx_len, prompt_slot)


def solution(mesh):
    placed = (
        P(("groups", "tensor", "batch"), None, None),
        P(None, "tensor"),
        P(None, "tensor"),
        P(("groups", "tensor", "batch"), None, None),
        P(("groups", "tensor", "batch"), None),
        P(("groups", "tensor", "batch")),
        P(("groups", "tensor", "batch")),
        P(("groups", "batch"), None, "tensor"),
    )
    return jax.shard_map(
        functools.partial(per_device, mesh.shape["tensor"]),
        mesh=mesh,
        in_specs=placed,
        out_specs=P(("groups", "tensor", "batch"), None, None),
        check_vma=False,
    )
```

```python
import functools

import jax
import jax.numpy as jnp
from jax import lax
from jax.experimental import pallas as pl
from jax.experimental.pallas import tpu as pltpu
from jax.sharding import PartitionSpec as P


QUERY_HEADS = 64
KEY_VALUE_HEADS = 8
HEAD_SIZE = 128
GROUP = QUERY_HEADS // KEY_VALUE_HEADS
STEPS = 2
MASKED = -1e30
PROJECT_LIMIT = 48 << 20
AHEAD = 3
LANES = 512
PAGES_AHEAD = 3
EARLY = 2
EARLY_LIMIT = 50 << 20
ATTEND_LIMIT = 50 << 20


def attend_kernel(
    table_ref, lens_ref, slot_ref, q_ref, kv_ref, prompt_ref, early_ref, pool_ref, out_ref,
    pages, q_pairs, new_scores, new_weights, acc, top_all, sum_all, q_f32, sems,
    *, seqs, q_width, kv_off, kv_width, prompt_width,
):
    span_pages = table_ref.shape[0] // seqs
    page_rows = pool_ref.shape[1]
    span = span_pages * page_rows
    early = early_ref.shape[0]
    rows = STEPS * GROUP
    new_rows = seqs * STEPS
    all_rows = KEY_VALUE_HEADS * rows
    pairs = KEY_VALUE_HEADS // 2
    wide = 2 * HEAD_SIZE
    value_at = KEY_VALUE_HEADS * HEAD_SIZE
    heads = range(KEY_VALUE_HEADS)

    def page_copy(s, p):
        return pltpu.make_async_copy(
            pool_ref.at[table_ref[s * span_pages + p]],
            pages.at[s - early, pl.ds(p * page_rows, page_rows)],
            sems.at[s - early, p],
        )

    for s in range(early, min(early + PAGES_AHEAD, seqs)):
        for p in range(span_pages):
            page_copy(s, p).start()

    def new_pair(col):
        block, at = col // kv_width, kv_off + col % kv_width
        return kv_ref[block, :, at : at + wide]

    def prompt_pair(col):
        block, at = col // prompt_width, col % prompt_width
        return prompt_ref[block, :, at : at + wide]

    def scaled(q, keys):
        return lax.dot_general(
            q, keys, (((1,), (1,)), ((), ())), preferred_element_type=jnp.float32
        ) * HEAD_SIZE ** (-0.5)

    def mix(w, values):
        return jnp.dot(w.astype(jnp.bfloat16), values, preferred_element_type=jnp.float32)

    for h in range(QUERY_HEADS):
        k, g = h // GROUP, h % GROUP
        block, at = (h * HEAD_SIZE) // q_width, (h * HEAD_SIZE) % q_width
        q_f32[k, pl.ds(g, new_rows, stride=GROUP), :] = q_ref[block, :, at : at + HEAD_SIZE].astype(jnp.float32)
    blank = jnp.zeros((seqs, rows, HEAD_SIZE), jnp.bfloat16)
    for k in heads:
        j, half = k // 2, k % 2
        mine = slice(half * rows, (half + 1) * rows)
        q_pairs[j, :, mine, half * HEAD_SIZE : (half + 1) * HEAD_SIZE] = (
            q_f32[k].astype(jnp.bfloat16).reshape(seqs, rows, HEAD_SIZE)
        )
        q_pairs[j, :, mine, (1 - half) * HEAD_SIZE : (2 - half) * HEAD_SIZE] = blank

    step_of = (lax.broadcasted_iota(jnp.int32, (seqs, 2 * rows, new_rows), 1) // GROUP) % STEPS
    seq_of = lax.broadcasted_iota(jnp.int32, (seqs, 2 * rows, new_rows), 0)
    offset = lax.broadcasted_iota(jnp.int32, (seqs, 2 * rows, new_rows), 2) - seq_of * STEPS
    live_new = (offset >= 0) & (offset <= step_of)
    for j in range(pairs):
        sn = scaled(q_pairs[j].reshape(seqs * 2 * rows, wide), new_pair(j * wide))
        new_scores[:, j * 2 * rows : (j + 1) * 2 * rows, :] = jnp.where(
            live_new, sn.reshape(seqs, 2 * rows, new_rows), MASKED
        )

    where_key = lax.broadcasted_iota(jnp.int32, (all_rows, span), 1)

    def context_of(s):
        if s < early:
            return early_ref.at[s]
        return pages.at[s - early]

    def cached_scores(s):
        if s >= early:
            if s + PAGES_AHEAD < seqs:
                for p in range(span_pages):
                    page_copy(s + PAGES_AHEAD, p).start()
            for p in range(span_pages):
                page_copy(s, p).wait()
        context = context_of(s)
        sc = jnp.concatenate(
            [scaled(q_pairs[j, s], context[:, j * wide : (j + 1) * wide]) for j in range(pairs)]
        )
        return jnp.where(where_key < lens_ref[s], sc, MASKED)

    def one_sequence(s, sc):
        part_rows = slice(s * rows, (s + 1) * rows)
        context = context_of(s)
        sn = new_scores[s]
        top = jnp.maximum(jnp.max(sc, axis=1, keepdims=True), jnp.max(sn, axis=1, keepdims=True))
        ec = jnp.exp(sc - top)
        en = jnp.exp(sn - top)
        total = jnp.sum(ec, axis=1, keepdims=True) + jnp.sum(en, axis=1, keepdims=True)
        new_weights[s] = en.astype(jnp.bfloat16)
        for j in range(pairs):
            col = value_at + j * wide
            both = mix(ec[j * 2 * rows : (j + 1) * 2 * rows], context[:, col : col + wide])
            acc[2 * j, part_rows, :] = both[:rows, :HEAD_SIZE]
            acc[2 * j + 1, part_rows, :] = both[rows:, HEAD_SIZE:]
        for k in heads:
            part = slice(k * rows, (k + 1) * rows)
            top_all[k, part_rows, :] = jnp.broadcast_to(top[part], (rows, HEAD_SIZE))
            sum_all[k, part_rows, :] = jnp.broadcast_to(total[part], (rows, HEAD_SIZE))

    scores = cached_scores(0)
    for s in range(seqs):
        following = cached_scores(s + 1) if s + 1 < seqs else None
        one_sequence(s, scores)
        scores = following

    for j in range(pairs):
        w = new_weights[:, j * 2 * rows : (j + 1) * 2 * rows, :].reshape(seqs * 2 * rows, new_rows)
        both = mix(w, new_pair(value_at + j * wide)).reshape(seqs, 2 * rows, wide)
        acc[2 * j] += both[:, :rows, :HEAD_SIZE].reshape(seqs * rows, HEAD_SIZE)
        acc[2 * j + 1] += both[:, rows:, HEAD_SIZE:].reshape(seqs * rows, HEAD_SIZE)

    slot = slot_ref[0]
    mine = pl.ds(pl.multiple_of(slot * rows, rows), rows)
    sp = jnp.concatenate([scaled(q_pairs[j, slot], prompt_pair(j * wide)) for j in range(pairs)])
    before = jnp.concatenate([top_all[k, mine, :] for k in heads])
    top = jnp.maximum(before, jnp.max(sp, axis=1, keepdims=True))
    ep = jnp.exp(sp - top[:, :1])
    keep = jnp.exp(before - top)
    more = jnp.sum(ep, axis=1, keepdims=True)
    for j in range(pairs):
        both = mix(ep[j * 2 * rows : (j + 1) * 2 * rows], prompt_pair(value_at + j * wide))
        for half in (0, 1):
            k = 2 * j + half
            part = slice(k * rows, (k + 1) * rows)
            added = both[half * rows : (half + 1) * rows, half * HEAD_SIZE : (half + 1) * HEAD_SIZE]
            sum_all[k, mine, :] = sum_all[k, mine, :] * keep[part] + more[part]
            acc[k, mine, :] = acc[k, mine, :] * keep[part] + added

    acc[...] = acc[...] / sum_all[...]
    for h in range(QUERY_HEADS):
        k, g = h // GROUP, h % GROUP
        head = acc[k, pl.ds(g, new_rows, stride=GROUP), :].astype(jnp.bfloat16)
        out_ref[:, :, h * HEAD_SIZE : (h + 1) * HEAD_SIZE] = head.reshape(seqs, STEPS, HEAD_SIZE)


def attend(joined, q_width, prompt, early, pool, table, lens, slot):
    blocks, tokens, width = joined.shape
    seqs = tokens // STEPS
    kv_width = width - q_width
    kv_off = q_width
    kv = joined
    if kv_width % (2 * HEAD_SIZE):
        kv = joined[:, :, q_width:].transpose(1, 0, 2).reshape(1, tokens, blocks * kv_width)
        prompt = prompt.transpose(1, 0, 2).reshape(1, prompt.shape[1], blocks * kv_width)
        kv_width, kv_off = blocks * kv_width, 0
    rows = seqs * STEPS * GROUP
    smem = pl.BlockSpec(memory_space=pltpu.SMEM)
    vmem = pl.BlockSpec(memory_space=pltpu.VMEM)
    kernel = functools.partial(
        attend_kernel, seqs=seqs, q_width=q_width, kv_off=kv_off, kv_width=kv_width, prompt_width=prompt.shape[2]
    )
    big = pltpu.VMEM((KEY_VALUE_HEADS, rows, HEAD_SIZE), jnp.float32)
    return pl.pallas_call(
        kernel,
        out_shape=jax.ShapeDtypeStruct((seqs, STEPS, QUERY_HEADS * HEAD_SIZE), jnp.bfloat16),
        in_specs=[smem, smem, smem, vmem, vmem, vmem, vmem, pl.BlockSpec(memory_space=pl.ANY)],
        out_specs=vmem,
        scratch_shapes=[
            pltpu.VMEM((seqs - early.shape[0], table.shape[1] * pool.shape[1], pool.shape[2]), jnp.bfloat16),
            pltpu.VMEM((KEY_VALUE_HEADS // 2, seqs, 2 * STEPS * GROUP, 2 * HEAD_SIZE), jnp.bfloat16),
            pltpu.VMEM((seqs, QUERY_HEADS * STEPS, tokens), jnp.float32),
            pltpu.VMEM((seqs, QUERY_HEADS * STEPS, tokens), jnp.bfloat16),
            big, big, big, big,
            pltpu.SemaphoreType.DMA((seqs - early.shape[0], table.shape[1])),
        ],
        compiler_params=pltpu.CompilerParams(vmem_limit_bytes=ATTEND_LIMIT),
        name="attend",
    )(table.reshape(-1), lens, slot, joined, kv, prompt, early, pool)


def early_kernel(table_ref, token_ref, pool_ref, out_ref, sems):
    page_rows = pool_ref.shape[1]
    each = out_ref.shape[1] // page_rows
    copies = [
        pltpu.make_async_copy(
            pool_ref.at[table_ref[s * each + p]], out_ref.at[s, pl.ds(p * page_rows, page_rows)], sems.at[s, p]
        )
        for s in range(out_ref.shape[0])
        for p in range(each)
    ]
    for c in copies:
        c.start()
    for c in copies:
        c.wait()


def early_pages(token, table, pool):
    seqs, each = min(EARLY, table.shape[0]), table.shape[1]
    hbm = pl.BlockSpec(memory_space=pl.ANY)
    shape = (seqs, each * pool.shape[1], pool.shape[2])
    return pl.pallas_call(
        early_kernel,
        out_shape=pltpu.VMEM(shape, pool.dtype),
        in_specs=[pl.BlockSpec(memory_space=pltpu.SMEM), hbm, hbm],
        out_specs=pl.BlockSpec(memory_space=pltpu.VMEM),
        scratch_shapes=[pltpu.SemaphoreType.DMA((seqs, each))],
        compiler_params=pltpu.CompilerParams(vmem_limit_bytes=EARLY_LIMIT),
        cost_estimate=pl.CostEstimate(flops=0, bytes_accessed=4 * shape[0] * shape[1] * shape[2], transcendentals=0),
        name="early",
    )(table.reshape(-1), token, pool)


def gather_blocks(own, axis, size):
    me = lax.axis_index(axis)
    line = size // 2
    place, side = me // 2, me % 2

    def hop(x, step, first, last):
        return lax.ppermute(
            x, axis, [(2 * c + p, 2 * (c + step) + p) for c in range(first, last + 1) for p in (0, 1)]
        )

    def swap(x, first, last):
        return lax.ppermute(x, axis, [(2 * c + p, 2 * c + 1 - p) for c in range(first, last + 1) for p in (0, 1)])

    up, down = {0: own}, {0: own}
    up_pair, down_pair = {}, {}
    near = swap(own, 0, line - 1)
    found = [((own,), 0, me), ((near,), 0, 2 * place + 1 - side)]
    for s in range(1, line - 1):
        up[s] = hop(up[s - 1], 1, s - 1, line - 2)
        down[s] = hop(down[s - 1], -1, 1, line - s)
        if s < line - 2:
            up_pair[s] = swap(up[s], s, line - 1)
            down_pair[s] = swap(down[s], 0, line - 1 - s)
    both = jnp.where(2 * place >= line, up[line - 2], down[line - 2])
    ends = [(1, 0), (line - 2, line - 1)]
    up[line - 1] = down[line - 1] = lax.ppermute(both, axis, [(2 * a + p, 2 * b + p) for a, b in ends for p in (0, 1)])
    up_pair[line - 2] = down_pair[line - 2] = lax.ppermute(
        both, axis, [(2 * c + p, 2 * c + 1 - p) for c in (0, 1, line - 2, line - 1) for p in (0, 1)]
    )
    up_pair[line - 1] = down_pair[line - 1] = lax.ppermute(
        up[line - 1], axis, [(2 * c + p, 2 * c + 1 - p) for c in (0, line - 1) for p in (0, 1)]
    )
    for s in range(1, line):
        other = (place + line - s) % line
        first = place >= s
        found.append(((up[s], down[line - s]), 1 - first.astype(jnp.int32), 2 * other + side))
        found.append(((up_pair[s], down_pair[line - s]), 1 - first.astype(jnp.int32), 2 * other + 1 - side))
    return found, (up[line - 1], down[line - 1])


def project_kernel(owner_ref, choice_ref, *refs, tiles, counts):
    blocks = sum(counts)
    sources = refs[:blocks]
    wq_ref, wkv_ref, out_ref, x_raw, x_here, x_sems, w_sems, *w_here = refs[blocks:]
    size, tokens, _ = out_ref.shape
    seqs = sources[0].shape[0]
    q_width = wq_ref.shape[1]

    def fetch(j, source):
        return pltpu.make_async_copy(source, x_raw.at[pl.ds(owner_ref[j] * seqs, seqs)], x_sems.at[j])

    at = 0
    firsts = []
    for j, count in enumerate(counts):
        firsts.append(sources[at])
        if count == 1:
            fetch(j, sources[at]).start()
        else:
            one, other = sources[at], sources[at + 1]

            @pl.when(choice_ref[j] == 0)
            def _():
                fetch(j, one).start()

            @pl.when(choice_ref[j] != 0)
            def _():
                fetch(j, other).start()

        at += count
    copies = []
    for i, (at, width) in enumerate(tiles):
        source = wq_ref.at[:, pl.ds(at, width)] if at < q_width else wkv_ref.at[:, pl.ds(at - q_width, width)]
        copies.append(pltpu.make_async_copy(source, w_here[i], w_sems.at[i]))
    for c in copies[:AHEAD]:
        c.start()
    for j, source in enumerate(firsts):
        fetch(j, source).wait()

    @pl.loop(0, x_raw.shape[2] // LANES)
    def _(c):
        cols = pl.ds(pl.multiple_of(c * LANES, LANES), LANES)
        x_here[:, cols] = x_raw[:, :, cols].reshape(size * tokens, LANES)

    for i, (at, width) in enumerate(tiles):
        copies[i].wait()
        if i + AHEAD < len(tiles):
            copies[i + AHEAD].start()
        cols = slice(at, at + width)
        y = jnp.dot(x_here[...], w_here[i][...], preferred_element_type=jnp.float32).astype(jnp.bfloat16)
        for j in range(size):
            out_ref[j, :, cols] = y[j * tokens : (j + 1) * tokens]


def project(found, wq, wkv):
    size = len(found)
    block = found[0][0][0].shape
    tokens = block[0] * block[1]
    depth, q_width = wq.shape
    width = q_width + wkv.shape[1]
    wide = 2 * HEAD_SIZE
    tiles = [(at, min(wide, q_width - at)) for at in range(0, q_width, wide)]
    tiles += [(at, min(wide, width - at)) for at in range(q_width, width, wide)]
    counts = [len(options) for options, _, _ in found]
    sources = [block for options, _, _ in found for block in options]
    choices = jnp.stack([jnp.asarray(choice, jnp.int32) for _, choice, _ in found])
    owners = jnp.stack([jnp.asarray(owner, jnp.int32) for _, _, owner in found])
    smem = pl.BlockSpec(memory_space=pltpu.SMEM)
    vmem = pl.BlockSpec(memory_space=pltpu.VMEM)
    hbm = pl.BlockSpec(memory_space=pl.ANY)
    return pl.pallas_call(
        functools.partial(project_kernel, tiles=tiles, counts=counts),
        out_shape=jax.ShapeDtypeStruct((size, tokens, width), jnp.bfloat16),
        in_specs=[smem, smem] + [hbm] * len(sources) + [hbm, hbm],
        out_specs=vmem,
        scratch_shapes=[
            pltpu.VMEM((size * block[0], block[1], depth), wq.dtype),
            pltpu.VMEM((size * tokens, depth), wq.dtype),
            pltpu.SemaphoreType.DMA((size,)),
            pltpu.SemaphoreType.DMA((len(tiles),)),
        ]
        + [pltpu.VMEM((depth, w), wq.dtype) for _, w in tiles],
        compiler_params=pltpu.CompilerParams(vmem_limit_bytes=PROJECT_LIMIT),
        cost_estimate=pl.CostEstimate(
            flops=2 * size * tokens * depth * width,
            bytes_accessed=2 * depth * (size * tokens + width),
            transcendentals=0,
        ),
        name="project",
    )(owners, choices, pltpu.with_memory_space_constraint(sources[0], pltpu.HBM), *sources[1:], wq, wkv)


def per_device(size, hidden, wq, wkv, cache_pool, page_table, ctx_len, prompt_slot, prompt_kv):
    found, late = gather_blocks(hidden, "tensor", size)
    prompt_kv, _ = lax.optimization_barrier((prompt_kv, late))
    prompt = lax.all_to_all(prompt_kv, "tensor", split_axis=0, concat_axis=0, tiled=True)
    joined = project(found, wq, wkv)
    joined, prompt = lax.optimization_barrier((joined, prompt))
    back = lax.all_to_all(joined, "tensor", split_axis=0, concat_axis=0, tiled=True)
    early = early_pages(joined, page_table, cache_pool)
    return attend(back, wq.shape[1], prompt, early, cache_pool, page_table, ctx_len, prompt_slot)


def solution(mesh):
    placed = (
        P(("groups", "tensor", "batch"), None, None),
        P(None, "tensor"),
        P(None, "tensor"),
        P(("groups", "tensor", "batch"), None, None),
        P(("groups", "tensor", "batch"), None),
        P(("groups", "tensor", "batch")),
        P(("groups", "tensor", "batch")),
        P(("groups", "batch"), None, "tensor"),
    )
    return jax.shard_map(
        functools.partial(per_device, mesh.shape["tensor"]),
        mesh=mesh,
        in_specs=placed,
        out_specs=P(("groups", "tensor", "batch"), None, None),
        check_vma=False,
    )
```
